32 devices in a mesh: obs: 4 (over y, core), flux: 8 (over z, x).
Axes of the slice: x: 2, y: 2, z: 4, core: 2. Of those that a mesh axis runs over, the one named last changes fastest.
Arguments:
- jacobian: bfloat16 [512, 8192], P('obs', 'flux'), may hold values from -0.0625 to 0.0625
- probes: bfloat16 [2, 8192, 128], P(None, 'flux'), may hold values from -6 to 6
- prior_std: float32 [8192], P('flux'), may hold values from 0.5 to 2
- obs_weight: float32 [512], P('obs'), may hold values from 0.25 to 4
Outputs:
- sketch: float32 [8192, 256], P(('flux', 'obs'))
- basis_out: float32 [8192, 256], P(('flux', 'obs'))
The draws below stay inside these ranges and needn't reach their ends.
All inputs are finite; a program needn't handle non-finite values.
Results may differ from the reference program's by a relative error of at most 0.005.
Values may be sent and summed in bfloat16 or wider, within the bound.
A program may use at most 64 MiB of HBM per device.

```python
import math
import jax
import jax.numpy as jnp
from jax import lax

P_SIZE = 128
NB = 2
OBS = 512
FLUX = 8192


def level_of(own_key, extent, shards, least, high):
    loudness, own = 1.0, jax.random.fold_in(own_key, 6)
    for axis_at, parts in shards:
        steps = jnp.exp(jax.random.uniform(jax.random.fold_in(own, axis_at), (parts,), jnp.float32, least / len(shards), high / len(shards)))
        loudness = loudness * jnp.repeat(steps, extent[axis_at] // parts).reshape([-1 if axis == axis_at else 1 for axis in range(len(extent))])
    return loudness


def noise(own_key, dims, scale, limit, pieces=(), dtype=jnp.bfloat16):
    entries = scale * jax.random.normal(own_key, dims, jnp.float32)
    if pieces:
        entries = entries * level_of(own_key, dims, pieces, -0.22, 0.18)
    return jnp.clip(entries, -limit, limit).astype(dtype)


def setup_inputs(seed: int = 0) -> dict:
    splits = jax.random.split(jax.random.key(seed), 5)
    return {
        "jacobian": noise(splits[0], (OBS, FLUX), FLUX ** -0.5, 0.0625, ((0, 4), (1, 8))),
        "probes": noise(splits[1], (NB, FLUX, P_SIZE), 1.0, 6.0, ((1, 8),)),
        "prior_std": jnp.clip(jnp.exp(math.log(2.0) - 1.3862944 * jax.random.uniform(splits[2], (FLUX,), jnp.float32) ** level_of(splits[2], (FLUX,), ((0, 8),), -0.2, 0.2)), 0.5, 2.0),
        "obs_weight": jnp.clip(jnp.exp(math.log(4.0) - 2.7725887 * jax.random.uniform(splits[3], (OBS,), jnp.float32) ** level_of(splits[3], (OBS,), ((0, 4),), -0.2, 0.2)), 0.25, 4.0),
    }


def reference(jacobian, probes, prior_std, obs_weight):
    column_total = NB * P_SIZE
    stacked = jnp.transpose(probes.astype(jnp.float32), (1, 0, 2)).reshape(FLUX, column_total)
    stacked = (stacked * prior_std[:, None]).astype(jnp.bfloat16)
    forward = jnp.dot(jacobian.astype(jnp.float32), stacked.astype(jnp.float32), preferred_element_type=jnp.float32)
    weighted = (forward * obs_weight[:, None]).astype(jnp.bfloat16)
    adjoint = lax.dot_general(jacobian.astype(jnp.float32), weighted.astype(jnp.float32), (((0,), (0,)), ((), ())), preferred_element_type=jnp.float32)
    sketch = adjoint * prior_std[:, None]
    gram_matrix = jnp.dot(sketch.T.astype(jnp.float32), sketch.astype(jnp.float32), precision=lax.Precision.HIGHEST, preferred_element_type=jnp.float32)
    factor = jnp.linalg.cholesky(gram_matrix)
    basis_out = jax.scipy.linalg.solve_triangular(factor, sketch.T, lower=True).T * math.sqrt(FLUX)
    return (sketch, basis_out)
```

```python
import functools
import math

import jax
import jax.numpy as jnp
from jax import lax
from jax.experimental import pallas as pl
from jax.experimental.pallas import tpu as pltpu
from jax.sharding import PartitionSpec as P

MESH = pl.DeviceIdType.MESH
HIGHEST = lax.Precision.HIGHEST
F32 = jnp.float32
BF16 = jnp.bfloat16
LANES = 128
PANEL = 64
TILE = 8


def each(lower, upper, step):
    if upper - lower <= 16:
        for value in range(lower, upper):
            step(value)
    else:
        lax.fori_loop(lower, upper, lambda value, carry: (step(value), carry)[1], 0)


def only(condition, step):
    if condition is True:
        step()
    else:
        pl.when(condition)(step)


def wait_bytes(ref, sem):
    pltpu.make_async_copy(ref, ref, sem).wait()


def column(row):
    return jnp.broadcast_to(row, (LANES, LANES)).T


def factor_rows(work, start, stop, width):
    index = lax.broadcasted_iota(jnp.int32, (TILE, LANES), 0)

    def spread(x, k):
        return jnp.broadcast_to(x[k : k + 1, :], x.shape)

    def columns(x, at):
        return [jnp.broadcast_to(x[:, at + j : at + j + 1], (TILE, LANES)) for j in range(TILE)]

    for first in range(start, stop, TILE):
        left = first // LANES * LANES
        right = width + left + LANES
        spans = [slice(s, s + LANES) for s in range(0, right - left, LANES)]
        top = work[first : first + TILE, left:right]
        cols = columns(top, first - left)
        parts = [top[:, span] for span in spans]
        steps = []
        diagonal = jnp.ones((TILE, LANES), F32)
        for k in range(TILE):
            pivot = spread(cols[k], k)
            diagonal = jnp.where(index == k, pivot, diagonal)
            inverse = 1.0 / pivot
            pivot_row = [spread(part, k) for part in parts]
            heads = [spread(col, k) for col in cols]
            steps.append((inverse, pivot_row, heads))
            if k < TILE - 1:
                multiplier = jnp.where(index > k, cols[k], 0.0) * inverse
                for j in range(k + 1, TILE):
                    cols[j] = cols[j] - multiplier * heads[j]
                parts = [part - multiplier * row for part, row in zip(parts, pivot_row)]
        for below in range(first + TILE, stop, TILE):
            tile = work[below : below + TILE, left:right]
            lower = columns(tile, first - left)
            pieces = [tile[:, span] for span in spans]
            for k, (inverse, pivot_row, heads) in enumerate(steps):
                multiplier = lower[k] * inverse
                for j in range(k + 1, TILE):
                    lower[j] = lower[j] - multiplier * heads[j]
                pieces = [piece - multiplier * row for piece, row in zip(pieces, pivot_row)]
            for span, piece in zip(spans, pieces):
                work[below : below + TILE, left + span.start : left + span.stop] = piece
        root = 1.0 / jnp.sqrt(diagonal)
        for span, part in zip(spans, parts):
            work[first : first + TILE, left + span.start : left + span.stop] = part * root


def take_out(work, start, stop, low, high, width):
    left = low // LANES * LANES
    right = width + (stop + LANES - 1) // LANES * LANES
    update = lax.dot_general(
        work[start:stop, left : (high + LANES - 1) // LANES * LANES],
        work[start:stop, left:right],
        (((0,), (0,)), ((), ())),
        precision=HIGHEST,
        preferred_element_type=F32,
    )
    work[low:high, left:right] = work[low:high, left:right] - update[low - left : high - left, :]


def kernel(
    sizes, jac_hbm, probes_hbm, std_hbm, weight_hbm, sketch_out, inverse_out,
    jac, probes, std, weight, load_sems, std_col, weight_col, stacked, jt, jrecv, fsend, frecv, wbuf,
    gsend, gpair, gchunk, grecv, gfull,
    tsend, tpair, tchunk, trecv, tfull, work, send_sems, recv_sems,
):
    n_obs, n_flux = sizes
    blocks, flux_local, probe_count = probes.shape
    obs_local = jac.shape[0]
    width = blocks * probe_count
    portion = flux_local // n_obs
    n_y = n_obs // 2
    chips = n_y * n_flux
    w_owners, w_rows = fsend.shape[0], fsend.shape[1]
    g_owners = gsend.shape[1]

    o, f = lax.axis_index("obs"), lax.axis_index("flux")
    core, y = lax.rem(o, 2), o // 2
    chip = y * n_flux + f
    partner = (o + 1 - 2 * core, f)
    w_mine = True if w_owners == n_flux else f < w_owners
    g_mine = True if g_owners == chips else chip < g_owners

    def on_chip(step, c):
        other = lax.rem(chip + step, chips)
        return other, ((other // n_flux) * 2 + c, lax.rem(other, n_flux))

    barrier = pltpu.get_barrier_semaphore()

    def greet(step):
        _, device = on_chip(step, core)
        pl.semaphore_signal(barrier, inc=1, device_id=device, device_id_type=MESH)

    def greet_other(step):
        _, device = on_chip(step, 1 - core)
        pl.semaphore_signal(barrier, inc=1, device_id=device, device_id_type=MESH)

    loads = [
        pltpu.make_async_copy(src, dst, load_sems.at[i])
        for i, (src, dst) in enumerate(
            ((std_hbm, std), (weight_hbm, weight), (probes_hbm, probes), (jac_hbm, jac))
        )
    ]
    for load in loads:
        load.start()
    each(1, chips, greet)
    each(0, chips, greet_other)
    loads[0].wait()
    loads[1].wait()
    for s in range(flux_local // LANES):
        part = slice(s * LANES, (s + 1) * LANES)
        std_col[part, :] = column(std[:, part])
    for s in range(obs_local // LANES):
        part = slice(s * LANES, (s + 1) * LANES)
        weight_col[part, :] = column(weight[:, part])
    loads[2].wait()
    for b in range(blocks):
        stacked[:, b * probe_count : (b + 1) * probe_count] = (
            probes[b].astype(F32) * std_col[...]
        ).astype(BF16)
    loads[3].wait()
    partial = jnp.dot(jac[...], stacked[...], preferred_element_type=F32)
    fsend[...] = partial.reshape(w_owners, w_rows, width)
    jt[...] = jac[...].T.reshape(n_obs, portion, obs_local)

    pl.semaphore_wait(barrier, 2 * chips - 1)

    def send(src, dst, number, device):
        copy = pltpu.make_async_remote_copy(
            src_ref=src, dst_ref=dst, send_sem=send_sems.at[number],
            recv_sem=recv_sems.at[number], device_id=device, device_id_type=MESH,
        )
        copy.start()
        return copy

    def send_forward(step):
        other = lax.rem(f + step, n_flux)
        only(
            True if w_owners == n_flux else other < w_owners,
            lambda: send(fsend.at[other], frecv.at[f], 0, (o, other)) and None,
        )

    each(1, n_flux, send_forward)

    def send_jacobian(step):
        other = lax.rem(o + step, n_obs)
        send(jt.at[other], jrecv.at[core, y], 1, (other, f))

    each(1, n_obs, send_jacobian)
    jrecv[core, y] = jt[o]

    def weigh():
        frecv[f] = fsend[f]
        wait_bytes(frecv.at[pl.ds(0, n_flux - 1)], recv_sems.at[0])
        rows = jnp.sum(frecv[...], axis=0)
        at = pl.ds(pl.multiple_of(f * w_rows, w_rows), w_rows)
        factor = jnp.concatenate([weight_col[at, :]] * (width // LANES), axis=1)
        mine = y * w_owners + f
        wbuf[core, mine] = (rows * factor).astype(BF16)

        def share(step):
            _, device = on_chip(step, core)
            send(wbuf.at[core, mine], wbuf.at[core, mine], 2, device)

        each(1, chips, share)

    only(w_mine, weigh)
    w_total = n_y * w_owners
    if w_mine is True:
        wait_bytes(wbuf.at[core, pl.ds(0, w_total - 1)], recv_sems.at[2])
    else:
        pl.when(w_mine)(lambda: wait_bytes(wbuf.at[core, pl.ds(0, w_total - 1)], recv_sems.at[2]))
        pl.when(f >= w_owners)(lambda: wait_bytes(wbuf.at[core], recv_sems.at[2]))
    across = send(wbuf.at[core], wbuf.at[core], 3, partner)

    wait_bytes(jt.at[pl.ds(0, n_obs - 1)], recv_sems.at[1])

    def adjoint(c):
        total = jnp.zeros((portion, width), F32)
        for row in range(n_y):
            piece = wbuf[c, row * w_owners : (row + 1) * w_owners].reshape(obs_local, width)
            total = total + jnp.dot(jrecv[c, row], piece, preferred_element_type=F32)
        return total

    own_half = adjoint(core)
    across.wait_recv()
    total = own_half + adjoint(1 - core)
    at = pl.ds(pl.multiple_of(o * portion, portion), portion)
    sketch = total * jnp.concatenate([std_col[at, :]] * (width // LANES), axis=1)
    sketch_out[...] = sketch
    half = width // 2

    def gram(low, high):
        return lax.dot_general(
            sketch[:, low : low + half], sketch[:, high : high + half],
            (((0,), (0,)), ((), ())), precision=HIGHEST, preferred_element_type=F32,
        )

    gsend[0] = gram(0, 0).reshape(gsend.shape[1:])
    gsend[1] = gram(0, half).reshape(gsend.shape[1:])
    pair = send(gsend.at[1 - core], gpair, 4, partner)
    tsend[...] = gram(half, half).reshape(tsend.shape)
    tpair_copy = send(tsend.at[1 - core], tpair, 8, partner)

    pair.wait_recv()
    gchunk[...] = gsend[core] + gpair[...]

    def send_gram(step):
        other, device = on_chip(step, core)
        only(
            True if g_owners == chips else other < g_owners,
            lambda: send(gchunk.at[other], grecv.at[chip], 5, device) and None,
        )

    each(1, chips, send_gram)

    tpair_copy.wait_recv()
    tchunk[...] = tsend[core] + tpair[...]
    t_owners = tchunk.shape[0]
    piece = chip // 2
    t_mine = (chip == 2 * piece + lax.rem(piece, 2)) & (piece < t_owners)

    def send_tail(step):
        owned = lax.rem(piece + step, t_owners)
        owner = 2 * owned + lax.rem(owned, 2)
        device = ((owner // n_flux) * 2 + core, lax.rem(owner, n_flux))
        only(
            owner != chip,
            lambda: send(tchunk.at[owned], trecv.at[chip], 9, device) and None,
        )

    each(0, t_owners, send_tail)

    def total_gram():
        grecv[chip] = gchunk[chip]
        wait_bytes(grecv.at[pl.ds(0, chips - 1)], recv_sems.at[5])
        gfull[core, chip] = jnp.sum(grecv[...], axis=0)

        def share(step):
            _, device = on_chip(step, core)
            send(gfull.at[core, chip], gfull.at[core, chip], 6, device)

        each(1, chips, share)

    only(g_mine, total_gram)
    work[:, width:] = (
        lax.broadcasted_iota(jnp.int32, (width, width), 0)
        == lax.broadcasted_iota(jnp.int32, (width, width), 1)
    ).astype(F32)

    def total_tail():
        trecv[chip] = tchunk[piece]
        wait_bytes(trecv.at[pl.ds(0, chips - 1)], recv_sems.at[9])
        tfull[core * t_owners + piece] = jnp.sum(trecv[...], axis=0)

        def share(step, c):
            _, device = on_chip(step, c)
            send(tfull.at[core * t_owners + piece], tfull.at[core * t_owners + piece], 10, device)

        each(1, chips, lambda step: share(step, core))
        each(0, chips, lambda step: share(step, 1 - core))

    if g_mine is True:
        wait_bytes(gfull.at[core, pl.ds(0, g_owners - 1)], recv_sems.at[6])
    else:
        pl.when(g_mine)(lambda: wait_bytes(gfull.at[core, pl.ds(0, g_owners - 1)], recv_sems.at[6]))
        pl.when(chip >= g_owners)(lambda: wait_bytes(gfull.at[core], recv_sems.at[6]))
    gacross = send(gfull.at[core], gfull.at[core], 7, partner)
    only(t_mine, total_tail)
    gacross.wait_recv()

    work[:half, :half] = gfull[0].reshape(half, half)
    work[:half, half:width] = gfull[1].reshape(half, half)
    for start in range(0, half, PANEL):
        factor_rows(work, start, start + PANEL, width)
        if start + PANEL < half:
            take_out(work, start, start + PANEL, start + PANEL, half, width)

    pl.when(t_mine)(lambda: wait_bytes(tfull.at[pl.ds(0, 2 * t_owners - 1)], recv_sems.at[10]))
    pl.when(jnp.logical_not(t_mine))(lambda: wait_bytes(tfull, recv_sems.at[10]))
    work[half:, half:width] = tfull[...].reshape(half, half)
    take_out(work, 0, half, half, width, width)
    for start in range(half, width, PANEL):
        factor_rows(work, start, start + PANEL, width)
        if start + PANEL < width:
            take_out(work, start, start + PANEL, start + PANEL, width, width)
    inverse_out[...] = work[:, width:]

    if w_mine is True:
        wait_bytes(fsend.at[pl.ds(0, w_owners - 1)], send_sems.at[0])
        wait_bytes(grecv.at[pl.ds(0, 0 + chips - 1)], send_sems.at[5])
    else:
        pl.when(w_mine)(lambda: wait_bytes(fsend.at[pl.ds(0, w_owners - 1)], send_sems.at[0]))
        pl.when(f >= w_owners)(lambda: wait_bytes(fsend, send_sems.at[0]))
        pl.when(g_mine)(lambda: wait_bytes(gchunk.at[pl.ds(0, g_owners - 1)], send_sems.at[5]))
        pl.when(chip >= g_owners)(lambda: wait_bytes(gchunk, send_sems.at[5]))
    wait_bytes(jt.at[pl.ds(0, n_obs - 1)], send_sems.at[1])

    def w_sent():
        each(1, chips, lambda step: wait_bytes(wbuf.at[core, 0], send_sems.at[2]))

    only(w_mine, w_sent)
    across.wait_send()
    pair.wait_send()

    def g_sent():
        each(1, chips, lambda step: wait_bytes(gfull.at[core, 0], send_sems.at[6]))

    only(g_mine, g_sent)
    gacross.wait_send()
    tpair_copy.wait_send()

    def tail_sent(count):
        each(0, count, lambda step: wait_bytes(tchunk.at[0], send_sems.at[9]))

    pl.when(t_mine)(lambda: tail_sent(t_owners - 1))
    pl.when(jnp.logical_not(t_mine))(lambda: tail_sent(t_owners))
    pl.when(t_mine)(
        lambda: each(1, 2 * chips, lambda step: wait_bytes(tchunk.at[0], send_sems.at[10]))
    )


def finish(scale, sketch, inverse, sketch_out, basis_out):
    sketch_out[...] = sketch[...]
    basis = lax.dot_general(
        sketch[...], inverse[...], (((1,), (1,)), ((), ())),
        precision=HIGHEST, preferred_element_type=F32,
    )
    basis_out[...] = basis * scale


def body(jacobian, probes, prior_std, obs_weight):
    blocks, flux_local, probe_count = probes.shape
    obs_local = jacobian.shape[0]
    n_obs, n_flux = lax.axis_size("obs"), lax.axis_size("flux")
    width = blocks * probe_count
    portion = flux_local // n_obs
    chips = n_obs // 2 * n_flux
    w_rows = max(16, obs_local // n_flux)
    w_owners = obs_local // w_rows
    half = width // 2
    g_rows = max(TILE, half // chips)
    g_owners = half // g_rows
    t_owners = half // 2 // TILE
    scale = math.sqrt(flux_local * n_flux)
    vmem = pl.BlockSpec(memory_space=pltpu.VMEM)
    out = jax.ShapeDtypeStruct((portion, width), F32)
    sketch, inverse = pl.pallas_call(
        functools.partial(kernel, (n_obs, n_flux)),
        out_shape=(out, jax.ShapeDtypeStruct((width, width), F32)),
        in_specs=[pl.BlockSpec(memory_space=pl.ANY)] * 4,
        out_specs=(vmem, vmem),
        scratch_shapes=[
            pltpu.VMEM(jacobian.shape, BF16),
            pltpu.VMEM(probes.shape, BF16),
            pltpu.VMEM((1, flux_local), F32),
            pltpu.VMEM((1, obs_local), F32),
            pltpu.SemaphoreType.DMA((4,)),
            pltpu.VMEM((flux_local, LANES), F32),
            pltpu.VMEM((obs_local, LANES), F32),
            pltpu.VMEM((flux_local, width), BF16),
            pltpu.VMEM((n_obs, portion, obs_local), BF16),
            pltpu.VMEM((2, n_obs // 2, portion, obs_local), BF16),
            pltpu.VMEM((w_owners, w_rows, width), F32),
            pltpu.VMEM((n_flux, w_rows, width), F32),
            pltpu.VMEM((2, n_obs // 2 * w_owners, w_rows, width), BF16),
            pltpu.VMEM((2, g_owners, g_rows, half), F32),
            pltpu.VMEM((g_owners, g_rows, half), F32),
            pltpu.VMEM((g_owners, g_rows, half), F32),
            pltpu.VMEM((chips, g_rows, half), F32),
            pltpu.VMEM((2, g_owners, g_rows, half), F32),
            pltpu.VMEM((2, t_owners, TILE, half), F32),
            pltpu.VMEM((t_owners, TILE, half), F32),
            pltpu.VMEM((t_owners, TILE, half), F32),
            pltpu.VMEM((chips, TILE, half), F32),
            pltpu.VMEM((2 * t_owners, TILE, half), F32),
            pltpu.VMEM((width, 2 * width), F32),
            pltpu.SemaphoreType.DMA((11,)),
            pltpu.SemaphoreType.DMA((11,)),
        ],
        compiler_params=pltpu.CompilerParams(collective_id=0, has_side_effects=True, vmem_limit_bytes=16 << 20),
    )(*[pltpu.with_memory_space_constraint(v, pltpu.HBM) for v in (jacobian, probes, prior_std.reshape(1, -1), obs_weight.reshape(1, -1))])
    return pl.pallas_call(
        functools.partial(finish, scale),
        out_shape=(out, out),
        in_specs=[vmem] * 2,
        out_specs=(vmem, vmem),
        compiler_params=pltpu.CompilerParams(vmem_limit_bytes=8 << 20),
    )(sketch, inverse)


def solution(mesh):
    in_specs = (P("obs", "flux"), P(None, "flux", None), P("flux"), P("obs"))
    out_specs = (P(("flux", "obs"), None), P(("flux", "obs"), None))
    return jax.shard_map(body, mesh=mesh, in_specs=in_specs, out_specs=out_specs, check_vma=False)
```

```python
import functools
import math

import jax
import jax.numpy as jnp
from jax import lax
from jax.experimental import pallas as pl
from jax.experimental.pallas import tpu as pltpu
from jax.sharding import PartitionSpec as P

MESH = pl.DeviceIdType.MESH
HIGHEST = lax.Precision.HIGHEST
F32 = jnp.float32
BF16 = jnp.bfloat16
LANES = 128
PANEL = 64
TILE = 8


def each(lower, upper, step):
    if upper - lower <= 16:
        for value in range(lower, upper):
            step(value)
    else:
        lax.fori_loop(lower, upper, lambda value, carry: (step(value), carry)[1], 0)


def wait_bytes(ref, sem):
    pltpu.make_async_copy(ref, ref, sem).wait()


def column(row):
    return jnp.broadcast_to(row, (LANES, LANES)).T


def spread(x, k):
    return jnp.broadcast_to(x[k : k + 1, :], (TILE, LANES))


def lane(x, c):
    return jnp.broadcast_to(x[:, c : c + 1], (TILE, LANES))


def eliminate(rows, offset):
    index = lax.broadcasted_iota(jnp.int32, (TILE, LANES), 0)
    count = len(rows)
    cols = [lane(rows[0][0], offset + j) for j in range(TILE)]
    for t in range(count):
        base = offset + t * TILE
        lows = {b: [lane(rows[b][0], base + j) for j in range(TILE)] for b in range(t + 1, count)}
        ahead = [lane(rows[t + 1][0], base + TILE + j) for j in range(TILE)] if t + 1 < count else []
        diagonal = jnp.ones((TILE, LANES), F32)
        for k in range(TILE):
            pivot = spread(cols[k], k)
            diagonal = jnp.where(index == k, pivot, diagonal)
            inverse = 1.0 / pivot
            lead = [spread(part, k) for part in rows[t]]
            heads = [spread(col, k) if j > k else None for j, col in enumerate(cols)]
            if k < TILE - 1:
                multiplier = jnp.where(index > k, cols[k], 0.0) * inverse
                for j in range(k + 1, TILE):
                    cols[j] = cols[j] - multiplier * heads[j]
                rows[t] = [part - multiplier * row for part, row in zip(rows[t], lead)]
            for b, low in lows.items():
                multiplier = low[k] * inverse
                if b == t + 1:
                    ahead = [a - multiplier * spread(low[k], j) for j, a in enumerate(ahead)]
                for j in range(k + 1, TILE):
                    low[j] = low[j] - multiplier * heads[j]
                rows[b] = [part - multiplier * row for part, row in zip(rows[b], lead)]
        root = lax.rsqrt(diagonal)
        rows[t] = [part * root for part in rows[t]]
        cols = ahead
    return rows


def factor(work):
    size = work.shape[0]
    spans = [slice(s, s + LANES) for s in range(0, 2 * size, LANES)]
    for start in range(0, size, PANEL):
        if start:
            update = lax.dot_general(
                work[start - PANEL : start, :size],
                work[start - PANEL : start, :],
                (((0,), (0,)), ((), ())),
                precision=HIGHEST,
                preferred_element_type=F32,
            )
            work[start:, :] = work[start:, :] - update[start:, :]
        rows = [
            [work[first : first + TILE, span] for span in spans]
            for first in range(start, start + PANEL, TILE)
        ]
        for t, row in enumerate(eliminate(rows, start)):
            first = start + t * TILE
            for span, part in zip(spans, row):
                work[first : first + TILE, span] = part


def identity(size):
    return (
        lax.broadcasted_iota(jnp.int32, (size, size), 0)
        == lax.broadcasted_iota(jnp.int32, (size, size), 1)
    ).astype(F32)


def halves(x):
    high = x.astype(BF16)
    return high, (x - high.astype(F32)).astype(BF16)


def kernel(
    sizes, scale, jac_hbm, probes_hbm, std_hbm, weight_hbm, sketch_out, basis_out, inverse_out,
    jac, probes, std, weight, load_sems, std_col, weight_col, stacked, jt, jrecv, fsend, frecv, wbuf,
    gsend, grecv, gfull, work, work_tail, send_sems, recv_sems,
):
    n_obs, n_flux = sizes
    blocks, flux_local, probe_count = probes.shape
    obs_local = jac.shape[0]
    width = blocks * probe_count
    half = width // 2
    portion = flux_local // n_obs
    n_y = n_obs // 2
    chips = n_y * n_flux
    chip_rows = 2 * portion
    w_owners, w_rows = fsend.shape[0], fsend.shape[1]
    w_first = (n_flux - w_owners) // 2
    g_owners = gsend.shape[1]
    g_row = max(1, g_owners // n_y)
    g_first = (n_flux - g_row) // 2

    o, f = lax.axis_index("obs"), lax.axis_index("flux")
    core, y = lax.rem(o, 2), o // 2
    chip = y * n_flux + f
    partner = (o + 1 - 2 * core, f)
    w_index = f - w_first
    w_mine = (w_index >= 0) & (w_index < w_owners)
    g_index = y * g_row + f - g_first
    g_mine = (f >= g_first) & (f < g_first + g_row) & (y < g_owners // g_row)

    def on_chip(step, c):
        other = lax.rem(chip + step, chips)
        return ((other // n_flux) * 2 + c, lax.rem(other, n_flux))

    loads = [
        pltpu.make_async_copy(src, dst, load_sems.at[i])
        for i, (src, dst) in enumerate(
            ((std_hbm, std), (weight_hbm, weight), (probes_hbm, probes), (jac_hbm, jac))
        )
    ]
    for load in loads:
        load.start()

    barrier = pltpu.get_barrier_semaphore()

    def greet(step, c):
        pl.semaphore_signal(
            barrier, inc=1, device_id=on_chip(step, c), device_id_type=MESH
        )

    each(1, chips, lambda step: greet(step, core))
    each(0, chips, lambda step: greet(step, 1 - core))

    loads[0].wait()
    loads[1].wait()
    for s in range(flux_local // LANES):
        part = slice(s * LANES, (s + 1) * LANES)
        std_col[part, :] = column(std[:, part])
    for s in range(obs_local // LANES):
        part = slice(s * LANES, (s + 1) * LANES)
        weight_col[part, :] = column(weight[:, part])
    loads[2].wait()
    for b in range(blocks):
        stacked[:, b * probe_count : (b + 1) * probe_count] = (
            probes[b].astype(F32) * std_col[...]
        ).astype(BF16)
    loads[3].wait()
    partial = jnp.dot(jac[...], stacked[...], preferred_element_type=F32)
    fsend[...] = partial.reshape(w_owners, w_rows, width)

    pl.semaphore_wait(barrier, 2 * chips - 1)

    def send(src, dst, number, device):
        copy = pltpu.make_async_remote_copy(
            src_ref=src, dst_ref=dst, send_sem=send_sems.at[number],
            recv_sem=recv_sems.at[number], device_id=device, device_id_type=MESH,
        )
        copy.start()
        return copy

    for j in range(w_owners):
        pl.when(w_index != j)(
            lambda j=j: send(fsend.at[j], frecv.at[f], 0, (o, w_first + j)) and None
        )

    jt[...] = jac[...].T

    def send_jacobian(step):
        other = lax.rem(o + step, n_obs)
        rows = pl.ds(pl.multiple_of((other // 2) * chip_rows, chip_rows), chip_rows)
        send(jt.at[rows], jrecv.at[core * n_y + y], 1, (other, f))

    each(1, n_obs, send_jacobian)
    chip_at = pl.ds(pl.multiple_of(y * chip_rows, chip_rows), chip_rows)
    jrecv[core * n_y + y] = jt[chip_at, :]

    @pl.when(w_mine)
    def _():
        frecv[f] = fsend[w_index]
        wait_bytes(frecv.at[pl.ds(0, n_flux - 1)], recv_sems.at[0])
        rows = jnp.sum(frecv[...], axis=0)
        at = pl.ds(pl.multiple_of(w_index * w_rows, w_rows), w_rows)
        by = jnp.concatenate([weight_col[at, :]] * (width // LANES), axis=1)
        mine = y * w_owners + w_index
        wbuf[core, mine] = (rows * by).astype(BF16)
        each(
            1, chips,
            lambda step: send(wbuf.at[core, mine], wbuf.at[core, mine], 2, on_chip(step, core)) and None,
        )
        wait_bytes(wbuf.at[core, pl.ds(0, n_y * w_owners - 1)], recv_sems.at[2])

    @pl.when(jnp.logical_not(w_mine))
    def _():
        wait_bytes(wbuf.at[core], recv_sems.at[2])

    across = send(wbuf.at[core], wbuf.at[core], 3, partner)
    wait_bytes(jrecv.at[pl.ds(0, n_obs - 1)], recv_sems.at[1])

    def adjoint(c):
        return jnp.dot(
            jnp.concatenate([jrecv[c * n_y + row] for row in range(n_y)], axis=1),
            wbuf[c].reshape(n_y * obs_local, width),
            preferred_element_type=F32,
        )

    own_half = adjoint(core)
    across.wait_recv()
    total = own_half + adjoint(1 - core)
    sketch = total * jnp.concatenate([std_col[chip_at, :]] * (width // LANES), axis=1)
    high, low = halves(sketch)

    def gram(first, upto):
        side = [x[:, first : first + half] for x in (high, low)]
        rest = [x[:, first:upto] for x in (high, low)]
        return lax.dot_general(
            jnp.concatenate([side[0], side[0], side[1]], axis=0),
            jnp.concatenate([rest[0], rest[1], rest[0]], axis=0),
            (((0,), (0,)), ((), ())), preferred_element_type=F32,
        )

    def pieces(block):
        return block.reshape(2, g_owners, TILE, half)

    def send_gram(number, parts):
        at = pl.ds(parts[0], len(parts))
        for j in range(g_owners):
            owner = (2 * (j // g_row) + core, g_first + j % g_row)
            pl.when((f != owner[1]) | (y != j // g_row))(
                lambda j=j, owner=owner: send(
                    gsend.at[core, j, at], grecv.at[chip, at], number, owner
                ) and None
            )

    leading = gram(0, width)
    gsend[:, :, 0] = pieces(leading[:, :half])
    send_gram(4, (0,))
    gsend[:, :, 1] = pieces(leading[:, half:])
    gsend[:, :, 2] = pieces(gram(half, width))
    send_gram(5, (1, 2))

    @pl.when(core == 0)
    def _():
        sketch_out[...] = sketch[:portion]

    @pl.when(core == 1)
    def _():
        sketch_out[...] = sketch[portion:]

    work[:, half:] = identity(half)
    work_tail[:, half:] = identity(half)

    @pl.when(g_mine)
    def _():
        for number, parts in ((4, (0,)), (5, (1, 2))):
            at = pl.ds(parts[0], len(parts))
            grecv[chip, at] = gsend[core, g_index, at]
            wait_bytes(grecv.at[pl.ds(0, chips - 1), at], recv_sems.at[number])
            gfull[core * g_owners + g_index, at] = jnp.sum(grecv[:, at], axis=0)

            def share(step, c, at=at, number=number):
                mine = gfull.at[core * g_owners + g_index, at]
                send(mine, mine, number + 2, on_chip(step, c))

            each(1, chips, lambda step: share(step, core))
            each(0, chips, lambda step: share(step, 1 - core))

    def arrived(number, parts):
        at = pl.ds(parts[0], len(parts))

        @pl.when(g_mine)
        def _():
            wait_bytes(gfull.at[pl.ds(0, 2 * g_owners - 1), at], recv_sems.at[number])

        @pl.when(jnp.logical_not(g_mine))
        def _():
            wait_bytes(gfull.at[:, at], recv_sems.at[number])

    arrived(6, (0,))
    work[:, :half] = gfull[:, 0].reshape(half, half)
    factor(work)
    arrived(7, (1, 2))
    inverse = work[:, half:]
    sketch = sketch_out[...]

    def product(a, b, dims):
        return lax.dot_general(
            a, b, (dims, ((), ())), precision=HIGHEST, preferred_element_type=F32
        )

    cross = product(inverse, gfull[:, 1].reshape(half, half), ((1,), (0,)))
    work_tail[:, :half] = gfull[:, 2].reshape(half, half) - product(cross, cross, ((0,), (0,)))
    first = product(sketch[:, :half], inverse, ((1,), (1,)))
    basis_out[:, :half] = first * scale
    basis_out[:, half:] = (sketch[:, half:] - product(first, cross, ((1,), (0,)))) * scale
    factor(work_tail)
    inverse_out[...] = work_tail[:, half:]

    for j in range(w_owners):
        pl.when(w_index != j)(lambda: wait_bytes(fsend.at[0], send_sems.at[0]))
    each(1, n_obs, lambda step: wait_bytes(jrecv.at[0], send_sems.at[1]))

    @pl.when(w_mine)
    def _():
        each(1, chips, lambda step: wait_bytes(wbuf.at[core, 0], send_sems.at[2]))

    across.wait_send()
    for number, parts in ((4, (0,)), (5, (1, 2))):
        at = pl.ds(parts[0], len(parts))
        each(0, g_owners - 1, lambda step: wait_bytes(gfull.at[0, at], send_sems.at[number]))
        pl.when(jnp.logical_not(g_mine))(
            lambda: wait_bytes(gfull.at[0, at], send_sems.at[number])
        )

        @pl.when(g_mine)
        def _():
            each(1, 2 * chips, lambda step: wait_bytes(gfull.at[0, at], send_sems.at[number + 2]))


def finish(sketch, basis, inverse, sketch_out, basis_out):
    half = inverse.shape[0]
    sketch_out[...] = sketch[...]
    basis_out[:, :half] = basis[:, :half]
    basis_out[:, half:] = lax.dot_general(
        basis[:, half:], inverse[...], (((1,), (1,)), ((), ())),
        precision=HIGHEST, preferred_element_type=F32,
    )


def body(jacobian, probes, prior_std, obs_weight):
    blocks, flux_local, probe_count = probes.shape
    obs_local = jacobian.shape[0]
    n_obs, n_flux = lax.axis_size("obs"), lax.axis_size("flux")
    width = blocks * probe_count
    half = width // 2
    portion = flux_local // n_obs
    n_y = n_obs // 2
    chips = n_y * n_flux
    w_rows = max(16, 2 * obs_local // n_flux)
    w_owners = obs_local // w_rows
    g_owners = half // 2 // TILE
    scale = math.sqrt(flux_local * n_flux)
    vmem = pl.BlockSpec(memory_space=pltpu.VMEM)
    out = jax.ShapeDtypeStruct((portion, width), F32)
    operands = (jacobian, probes, prior_std.reshape(1, -1), obs_weight.reshape(1, -1))
    sketch, basis, inverse = pl.pallas_call(
        functools.partial(kernel, (n_obs, n_flux), scale),
        out_shape=(out, out, jax.ShapeDtypeStruct((half, half), F32)),
        in_specs=[pl.BlockSpec(memory_space=pl.ANY)] * 4,
        out_specs=(vmem, vmem, vmem),
        scratch_shapes=[
            pltpu.VMEM(jacobian.shape, BF16),
            pltpu.VMEM(probes.shape, BF16),
            pltpu.VMEM((1, flux_local), F32),
            pltpu.VMEM((1, obs_local), F32),
            pltpu.SemaphoreType.DMA((4,)),
            pltpu.VMEM((flux_local, LANES), F32),
            pltpu.VMEM((obs_local, LANES), F32),
            pltpu.VMEM((flux_local, width), BF16),
            pltpu.VMEM((flux_local, obs_local), BF16),
            pltpu.VMEM((n_obs, 2 * portion, obs_local), BF16),
            pltpu.VMEM((w_owners, w_rows, width), F32),
            pltpu.VMEM((n_flux, w_rows, width), F32),
            pltpu.VMEM((2, n_y * w_owners, w_rows, width), BF16),
            pltpu.VMEM((2, g_owners, 3, TILE, half), F32),
            pltpu.VMEM((chips, 3, TILE, half), F32),
            pltpu.VMEM((2 * g_owners, 3, TILE, half), F32),
            pltpu.VMEM((half, width), F32),
            pltpu.VMEM((half, width), F32),
            pltpu.SemaphoreType.DMA((8,)),
            pltpu.SemaphoreType.DMA((8,)),
        ],
        compiler_params=pltpu.CompilerParams(
            collective_id=0, has_side_effects=True, vmem_limit_bytes=24 << 20
        ),
    )(*[pltpu.with_memory_space_constraint(x, pltpu.HBM) for x in operands])
    return pl.pallas_call(
        finish,
        out_shape=(out, out),
        in_specs=[vmem] * 3,
        out_specs=(vmem, vmem),
        compiler_params=pltpu.CompilerParams(vmem_limit_bytes=8 << 20),
    )(sketch, basis, inverse)


def solution(mesh):
    in_specs = (P("obs", "flux"), P(None, "flux", None), P("flux"), P("obs"))
    out_specs = (P(("flux", "obs"), None), P(("flux", "obs"), None))
    return jax.shard_map(body, mesh=mesh, in_specs=in_specs, out_specs=out_specs, check_vma=False)
```

```python
import functools
import math

import jax
import jax.numpy as jnp
from jax import lax
from jax.experimental import pallas as pl
from jax.experimental.pallas import tpu as pltpu
from jax.sharding import PartitionSpec as P

MESH = pl.DeviceIdType.MESH
HIGHEST = lax.Precision.HIGHEST
F32 = jnp.float32
BF16 = jnp.bfloat16
LANES = 128
PANEL = 64
TILE = 8


def each(lower, upper, step):
    if upper - lower <= 32:
        for value in range(lower, upper):
            step(value)
    else:
        lax.fori_loop(lower, upper, lambda value, carry: (step(value), carry)[1], 0)


def wait_bytes(ref, sem):
    pltpu.make_async_copy(ref, ref, sem).wait()


def column(row):
    return jnp.broadcast_to(row, (LANES, LANES)).T


def spread(x, k):
    return jnp.broadcast_to(x[k : k + 1, :], (TILE, LANES))


def lane(x, c):
    return jnp.broadcast_to(x[:, c : c + 1], (TILE, LANES))


def eliminate(rows, offset):
    index = lax.broadcasted_iota(jnp.int32, (TILE, LANES), 0)
    count = len(rows)
    cols = [lane(rows[0][0], offset + j) for j in range(TILE)]
    for t in range(count):
        base = offset + t * TILE
        lows = {b: [lane(rows[b][0], base + j) for j in range(TILE)] for b in range(t + 1, count)}
        ahead = [lane(rows[t + 1][0], base + TILE + j) for j in range(TILE)] if t + 1 < count else []
        diagonal = jnp.ones((TILE, LANES), F32)
        for k in range(TILE):
            pivot = spread(cols[k], k)
            diagonal = jnp.where(index == k, pivot, diagonal)
            inverse = 1.0 / pivot
            lead = [spread(part, k) for part in rows[t]]
            heads = [spread(col, k) if j > k else None for j, col in enumerate(cols)]
            if k < TILE - 1:
                multiplier = jnp.where(index > k, cols[k], 0.0) * inverse
                for j in range(k + 1, TILE):
                    cols[j] = cols[j] - multiplier * heads[j]
                rows[t] = [part - multiplier * row for part, row in zip(rows[t], lead)]
            for b, low in lows.items():
                multiplier = low[k] * inverse
                if b == t + 1:
                    ahead = [a - multiplier * spread(low[k], j) for j, a in enumerate(ahead)]
                for j in range(k + 1, TILE):
                    low[j] = low[j] - multiplier * heads[j]
                rows[b] = [part - multiplier * row for part, row in zip(rows[b], lead)]
        root = lax.rsqrt(diagonal)
        rows[t] = [part * root for part in rows[t]]
        cols = ahead
    return rows


def factor(work):
    size = work.shape[0]
    spans = [slice(s, s + LANES) for s in range(0, 2 * size, LANES)]
    for start in range(0, size, PANEL):
        if start:
            update = lax.dot_general(
                work[start - PANEL : start, :size],
                work[start - PANEL : start, :],
                (((0,), (0,)), ((), ())),
                precision=HIGHEST,
                preferred_element_type=F32,
            )
            work[start:, :] = work[start:, :] - update[start:, :]
        rows = [
            [work[first : first + TILE, span] for span in spans]
            for first in range(start, start + PANEL, TILE)
        ]
        for t, row in enumerate(eliminate(rows, start)):
            first = start + t * TILE
            for span, part in zip(spans, row):
                work[first : first + TILE, span] = part


def identity(size):
    return (
        lax.broadcasted_iota(jnp.int32, (size, size), 0)
        == lax.broadcasted_iota(jnp.int32, (size, size), 1)
    ).astype(F32)


def halves(x):
    high = x.astype(BF16)
    return high, (x - high.astype(F32)).astype(BF16)


def kernel(
    sizes, scale, jac_hbm, probes_hbm, std_hbm, weight_hbm, sketch_out, basis_out, inverse_out,
    jac, probes, std, weight, load_sems, std_col, weight_col, stacked, jt, jrecv, fsend, frecv, wbuf,
    gsend, grecv, gfull, work, work_tail, ready, send_sems, recv_sems,
):
    n_obs, n_flux = sizes
    blocks, flux_local, probe_count = probes.shape
    obs_local = jac.shape[0]
    width = blocks * probe_count
    half = width // 2
    portion = flux_local // n_obs
    n_y = n_obs // 2
    chips = n_y * n_flux
    chip_rows = 2 * portion
    w_owners, w_rows = fsend.shape[0], fsend.shape[1]
    w_first = (n_flux - w_owners) // 2
    g_owners = gsend.shape[1]
    g_row = max(1, g_owners // n_y)
    g_first = (n_flux - g_row) // 2

    o, f = lax.axis_index("obs"), lax.axis_index("flux")
    core, y = lax.rem(o, 2), o // 2
    chip = y * n_flux + f
    partner = (o + 1 - 2 * core, f)
    w_index = f - w_first
    w_mine = (w_index >= 0) & (w_index < w_owners)
    g_index = y * g_row + f - g_first
    g_mine = (f >= g_first) & (f < g_first + g_row) & (y < g_owners // g_row)

    def on_chip(step, c):
        other = lax.rem(chip + step, chips)
        return ((other // n_flux) * 2 + c, lax.rem(other, n_flux))

    loads = [
        pltpu.make_async_copy(src, dst, load_sems.at[i])
        for i, (src, dst) in enumerate(
            ((std_hbm, std), (weight_hbm, weight), (probes_hbm, probes), (jac_hbm, jac))
        )
    ]
    for load in loads:
        load.start()

    barrier = pltpu.get_barrier_semaphore()

    def signal(sem, device):
        pl.semaphore_signal(sem, inc=1, device_id=device, device_id_type=MESH)

    @pl.when(w_mine)
    def _():
        def greet(step):
            other = lax.rem(o * n_flux + f + step, n_obs * n_flux)
            signal(barrier, (other // n_flux, lax.rem(other, n_flux)))

        each(1, n_obs * n_flux, greet)

    @pl.when(jnp.logical_not(w_mine))
    def _():
        each(1, n_obs, lambda step: signal(barrier, (lax.rem(o + step, n_obs), f)))

    loads[0].wait()
    loads[1].wait()
    for s in range(flux_local // LANES):
        part = slice(s * LANES, (s + 1) * LANES)
        std_col[part, :] = column(std[:, part])
    for s in range(obs_local // LANES):
        part = slice(s * LANES, (s + 1) * LANES)
        weight_col[part, :] = column(weight[:, part])
    loads[2].wait()
    for b in range(blocks):
        stacked[:, b * probe_count : (b + 1) * probe_count] = (
            probes[b].astype(F32) * std_col[...]
        ).astype(BF16)
    loads[3].wait()
    partial = jnp.dot(jac[...], stacked[...], preferred_element_type=F32)
    fsend[...] = partial.reshape(w_owners, w_rows, width)

    hubs = n_obs * w_owners
    pl.when(w_mine)(lambda: pl.semaphore_wait(barrier, hubs - 1))
    pl.when(jnp.logical_not(w_mine))(lambda: pl.semaphore_wait(barrier, hubs + n_obs - 1))

    def send(src, dst, number, device):
        copy = pltpu.make_async_remote_copy(
            src_ref=src, dst_ref=dst, send_sem=send_sems.at[number],
            recv_sem=recv_sems.at[number], device_id=device, device_id_type=MESH,
        )
        copy.start()
        return copy

    for j in range(w_owners):
        pl.when(w_index != j)(
            lambda j=j: send(fsend.at[j], frecv.at[f], 0, (o, w_first + j)) and None
        )

    @pl.when(jnp.logical_not(w_mine))
    def _():
        each(0, hubs, lambda step: signal(ready, (step % n_obs, w_first + step // n_obs)))

    jt[...] = jac[...].T

    def send_jacobian(step):
        other = lax.rem(o + step, n_obs)
        rows = pl.ds(pl.multiple_of((other // 2) * chip_rows, chip_rows), chip_rows)
        send(jt.at[rows], jrecv.at[core * n_y + y], 1, (other, f))

    each(1, n_obs, send_jacobian)
    chip_at = pl.ds(pl.multiple_of(y * chip_rows, chip_rows), chip_rows)
    jrecv[core * n_y + y] = jt[chip_at, :]

    @pl.when(w_mine)
    def _():
        frecv[f] = fsend[w_index]
        wait_bytes(frecv.at[pl.ds(0, n_flux - 1)], recv_sems.at[0])
        rows = jnp.sum(frecv[...], axis=0)
        at = pl.ds(pl.multiple_of(w_index * w_rows, w_rows), w_rows)
        by = jnp.concatenate([weight_col[at, :]] * (width // LANES), axis=1)
        mine = y * w_owners + w_index
        wbuf[core, mine] = (rows * by).astype(BF16)
        pl.semaphore_wait(ready, n_obs * (n_flux - w_owners))
        each(
            1, chips,
            lambda step: send(wbuf.at[core, mine], wbuf.at[core, mine], 2, on_chip(step, core)) and None,
        )
        wait_bytes(wbuf.at[core, pl.ds(0, n_y * w_owners - 1)], recv_sems.at[2])

    @pl.when(jnp.logical_not(w_mine))
    def _():
        wait_bytes(wbuf.at[core], recv_sems.at[2])

    across = send(wbuf.at[core], wbuf.at[core], 3, partner)
    wait_bytes(jrecv.at[pl.ds(0, n_obs - 1)], recv_sems.at[1])

    def adjoint(c):
        return jnp.dot(
            jnp.concatenate([jrecv[c * n_y + row] for row in range(n_y)], axis=1),
            wbuf[c].reshape(n_y * obs_local, width),
            preferred_element_type=F32,
        )

    own_half = adjoint(core)
    across.wait_recv()
    total = own_half + adjoint(1 - core)
    sketch = total * jnp.concatenate([std_col[chip_at, :]] * (width // LANES), axis=1)
    high, low = halves(sketch)

    def gram(first, upto):
        side = [x[:, first : first + half] for x in (high, low)]
        rest = [x[:, first:upto] for x in (high, low)]
        return lax.dot_general(
            jnp.concatenate([side[0], side[0], side[1]], axis=0),
            jnp.concatenate([rest[0], rest[1], rest[0]], axis=0),
            (((0,), (0,)), ((), ())), preferred_element_type=F32,
        )

    def pieces(block):
        return block.reshape(2, g_owners, TILE, half)

    def send_gram(number, parts):
        at = pl.ds(parts[0], len(parts))
        for j in range(g_owners):
            owner = (2 * (j // g_row) + core, g_first + j % g_row)
            pl.when((f != owner[1]) | (y != j // g_row))(
                lambda j=j, owner=owner: send(
                    gsend.at[core, j, at], grecv.at[chip, at], number, owner
                ) and None
            )

    leading = gram(0, width)
    gsend[:, :, 0] = pieces(leading[:, :half])
    send_gram(4, (0,))
    gsend[:, :, 1] = pieces(leading[:, half:])
    gsend[:, :, 2] = pieces(gram(half, width))
    send_gram(5, (1, 2))

    @pl.when(core == 0)
    def _():
        sketch_out[...] = sketch[:portion]

    @pl.when(core == 1)
    def _():
        sketch_out[...] = sketch[portion:]

    work[:, half:] = identity(half)
    work_tail[:, half:] = identity(half)

    @pl.when(g_mine)
    def _():
        for number, parts in ((4, (0,)), (5, (1, 2))):
            at = pl.ds(parts[0], len(parts))
            grecv[chip, at] = gsend[core, g_index, at]
            wait_bytes(grecv.at[pl.ds(0, chips - 1), at], recv_sems.at[number])
            gfull[core * g_owners + g_index, at] = jnp.sum(grecv[:, at], axis=0)

            def share(step, at=at, number=number):
                mine = gfull.at[core * g_owners + g_index, at]
                to = (step % n_obs, step // n_obs)
                pl.when((o != to[0]) | (f != to[1]))(
                    lambda: send(mine, mine, number + 2, to) and None
                )

            each(0, n_obs * n_flux, share)

    def arrived(number, parts):
        at = pl.ds(parts[0], len(parts))

        @pl.when(g_mine)
        def _():
            wait_bytes(gfull.at[pl.ds(0, 2 * g_owners - 1), at], recv_sems.at[number])

        @pl.when(jnp.logical_not(g_mine))
        def _():
            wait_bytes(gfull.at[:, at], recv_sems.at[number])

    arrived(6, (0,))
    work[:, :half] = gfull[:, 0].reshape(half, half)
    factor(work)
    arrived(7, (1, 2))
    inverse = work[:, half:]
    sketch = sketch_out[...]

    def product(a, b, dims):
        return lax.dot_general(
            a, b, (dims, ((), ())), precision=HIGHEST, preferred_element_type=F32
        )

    cross = product(inverse, gfull[:, 1].reshape(half, half), ((1,), (0,)))
    work_tail[:, :half] = gfull[:, 2].reshape(half, half) - product(cross, cross, ((0,), (0,)))
    first = product(sketch[:, :half], inverse, ((1,), (1,)))
    basis_out[:, :half] = first * scale
    basis_out[:, half:] = (sketch[:, half:] - product(first, cross, ((1,), (0,)))) * scale
    factor(work_tail)
    inverse_out[...] = work_tail[:, half:]

    for j in range(w_owners):
        pl.when(w_index != j)(lambda: wait_bytes(fsend.at[0], send_sems.at[0]))
    each(1, n_obs, lambda step: wait_bytes(jrecv.at[0], send_sems.at[1]))

    @pl.when(w_mine)
    def _():
        each(1, chips, lambda step: wait_bytes(wbuf.at[core, 0], send_sems.at[2]))

    across.wait_send()
    for number, parts in ((4, (0,)), (5, (1, 2))):
        at = pl.ds(parts[0], len(parts))
        each(0, g_owners - 1, lambda step: wait_bytes(gfull.at[0, at], send_sems.at[number]))
        pl.when(jnp.logical_not(g_mine))(
            lambda: wait_bytes(gfull.at[0, at], send_sems.at[number])
        )

        @pl.when(g_mine)
        def _():
            each(1, 2 * chips, lambda step: wait_bytes(gfull.at[0, at], send_sems.at[number + 2]))


def finish(sketch, basis, inverse, sketch_out, basis_out):
    half = inverse.shape[0]
    sketch_out[...] = sketch[...]
    basis_out[:, :half] = basis[:, :half]
    basis_out[:, half:] = lax.dot_general(
        basis[:, half:], inverse[...], (((1,), (1,)), ((), ())),
        precision=HIGHEST, preferred_element_type=F32,
    )


def body(jacobian, probes, prior_std, obs_weight):
    blocks, flux_local, probe_count = probes.shape
    obs_local = jacobian.shape[0]
    n_obs, n_flux = lax.axis_size("obs"), lax.axis_size("flux")
    width = blocks * probe_count
    half = width // 2
    portion = flux_local // n_obs
    n_y = n_obs // 2
    chips = n_y * n_flux
    w_rows = max(16, 2 * obs_local // n_flux)
    w_owners = obs_local // w_rows
    g_owners = half // 2 // TILE
    scale = math.sqrt(flux_local * n_flux)
    vmem = pl.BlockSpec(memory_space=pltpu.VMEM)
    out = jax.ShapeDtypeStruct((portion, width), F32)
    operands = (jacobian, probes, prior_std.reshape(1, -1), obs_weight.reshape(1, -1))
    sketch, basis, inverse = pl.pallas_call(
        functools.partial(kernel, (n_obs, n_flux), scale),
        out_shape=(out, out, jax.ShapeDtypeStruct((half, half), F32)),
        in_specs=[pl.BlockSpec(memory_space=pl.ANY)] * 4,
        out_specs=(vmem, vmem, vmem),
        scratch_shapes=[
            pltpu.VMEM(jacobian.shape, BF16),
            pltpu.VMEM(probes.shape, BF16),
            pltpu.VMEM((1, flux_local), F32),
            pltpu.VMEM((1, obs_local), F32),
            pltpu.SemaphoreType.DMA((4,)),
            pltpu.VMEM((flux_local, LANES), F32),
            pltpu.VMEM((obs_local, LANES), F32),
            pltpu.VMEM((flux_local, width), BF16),
            pltpu.VMEM((flux_local, obs_local), BF16),
            pltpu.VMEM((n_obs, 2 * portion, obs_local), BF16),
            pltpu.VMEM((w_owners, w_rows, width), F32),
            pltpu.VMEM((n_flux, w_rows, width), F32),
            pltpu.VMEM((2, n_y * w_owners, w_rows, width), BF16),
            pltpu.VMEM((2, g_owners, 3, TILE, half), F32),
            pltpu.VMEM((chips, 3, TILE, half), F32),
            pltpu.VMEM((2 * g_owners, 3, TILE, half), F32),
            pltpu.VMEM((half, width), F32),
            pltpu.VMEM((half, width), F32),
            pltpu.SemaphoreType.REGULAR,
            pltpu.SemaphoreType.DMA((8,)),
            pltpu.SemaphoreType.DMA((8,)),
        ],
        compiler_params=pltpu.CompilerParams(
            collective_id=0, has_side_effects=True, vmem_limit_bytes=24 << 20
        ),
    )(*[pltpu.with_memory_space_constraint(x, pltpu.HBM) for x in operands])
    return pl.pallas_call(
        finish,
        out_shape=(out, out),
        in_specs=[vmem] * 3,
        out_specs=(vmem, vmem),
        compiler_params=pltpu.CompilerParams(vmem_limit_bytes=8 << 20),
    )(sketch, basis, inverse)


def solution(mesh):
    in_specs = (P("obs", "flux"), P(None, "flux", None), P("flux"), P("obs"))
    out_specs = (P(("flux", "obs"), None), P(("flux", "obs"), None))
    return jax.shard_map(body, mesh=mesh, in_specs=in_specs, out_specs=out_specs, check_vma=False)
```

```python
import functools
import math

import jax
import jax.numpy as jnp
from jax import lax
from jax.experimental import pallas as pl
from jax.experimental.pallas import tpu as pltpu
from jax.sharding import PartitionSpec as P

MESH = pl.DeviceIdType.MESH
HIGHEST = lax.Precision.HIGHEST
F32 = jnp.float32
BF16 = jnp.bfloat16
LANES = 128
PANEL = 64
TILE = 8


def each(lower, upper, step):
    if upper - lower <= 32:
        for value in range(lower, upper):
            step(value)
    else:
        lax.fori_loop(lower, upper, lambda value, carry: (step(value), carry)[1], 0)


def wait_bytes(ref, sem):
    pltpu.make_async_copy(ref, ref, sem).wait()


def column(row):
    return jnp.broadcast_to(row, (LANES, LANES)).T


def spread(x, k):
    return jnp.broadcast_to(x[k : k + 1, :], (TILE, LANES))


def lane(x, c):
    return jnp.broadcast_to(x[:, c : c + 1], (TILE, LANES))


def eliminate(rows, offset):
    index = lax.broadcasted_iota(jnp.int32, (TILE, LANES), 0)
    count = len(rows)
    cols = [lane(rows[0][0], offset + j) for j in range(TILE)]
    for t in range(count):
        base = offset + t * TILE
        lows = {b: [lane(rows[b][0], base + j) for j in range(TILE)] for b in range(t + 1, count)}
        ahead = [lane(rows[t + 1][0], base + TILE + j) for j in range(TILE)] if t + 1 < count else []
        diagonal = jnp.ones((TILE, LANES), F32)
        for k in range(TILE):
            pivot = spread(cols[k], k)
            diagonal = jnp.where(index == k, pivot, diagonal)
            inverse = 1.0 / pivot
            lead = [spread(part, k) for part in rows[t]]
            heads = [spread(col, k) if j > k else None for j, col in enumerate(cols)]
            if k < TILE - 1:
                multiplier = jnp.where(index > k, cols[k], 0.0) * inverse
                for j in range(k + 1, TILE):
                    cols[j] = cols[j] - multiplier * heads[j]
                rows[t] = [part - multiplier * row for part, row in zip(rows[t], lead)]
            for b, low in lows.items():
                multiplier = low[k] * inverse
                if b == t + 1:
                    ahead = [a - multiplier * spread(low[k], j) for j, a in enumerate(ahead)]
                for j in range(k + 1, TILE):
                    low[j] = low[j] - multiplier * heads[j]
                rows[b] = [part - multiplier * row for part, row in zip(rows[b], lead)]
        root = lax.rsqrt(diagonal)
        rows[t] = [part * root for part in rows[t]]
        cols = ahead
    return rows


def factor(work):
    size = work.shape[0]
    spans = [slice(s, s + LANES) for s in range(0, 2 * size, LANES)]
    for start in range(0, size, PANEL):
        if start:
            update = lax.dot_general(
                work[start - PANEL : start, :size],
                work[start - PANEL : start, :],
                (((0,), (0,)), ((), ())),
                precision=HIGHEST,
                preferred_element_type=F32,
            )
            work[start:, :] = work[start:, :] - update[start:, :]
        rows = [
            [work[first : first + TILE, span] for span in spans]
            for first in range(start, start + PANEL, TILE)
        ]
        for t, row in enumerate(eliminate(rows, start)):
            first = start + t * TILE
            for span, part in zip(spans, row):
                work[first : first + TILE, span] = part


def identity(size):
    return (
        lax.broadcasted_iota(jnp.int32, (size, size), 0)
        == lax.broadcasted_iota(jnp.int32, (size, size), 1)
    ).astype(F32)


def halves(x):
    high = x.astype(BF16)
    return high, (x - high.astype(F32)).astype(BF16)


def kernel(
    sizes, scale, jac_hbm, probes_hbm, std_hbm, weight_hbm, sketch_out, basis_out, inverse_out,
    jac, probes, std, weight, load_sems, std_col, weight_col, jt, jrecv, fsend, frecv, wbuf,
    gsend, grecv, gfull, work, work_tail, ready, send_sems, recv_sems,
):
    n_obs, n_flux = sizes
    blocks, flux_local, probe_count = probes.shape
    obs_local = jac.shape[0]
    width = blocks * probe_count
    half = probe_count
    portion = flux_local // n_obs
    n_y = n_obs // 2
    chips = n_y * n_flux
    chip_rows = 2 * portion
    w_owners, w_rows = fsend.shape[1], fsend.shape[2]
    w_first = (n_flux - w_owners) // 2
    g_owners = gsend.shape[1]
    g_row = max(1, g_owners // n_y)
    center = (n_flux - g_row) // 2
    waves = ((7, 0, 1, max(center - 1, 0)), (8, 1, 2, center))
    h_first = min(w_first, waves[0][3], waves[1][3])
    h_count = max(w_first + w_owners, waves[0][3] + g_row, waves[1][3] + g_row) - h_first

    o, f = lax.axis_index("obs"), lax.axis_index("flux")
    core, y = lax.rem(o, 2), o // 2
    hub = (f >= h_first) & (f < h_first + h_count)
    chip = y * n_flux + f
    partner = (o + 1 - 2 * core, f)
    w_index = f - w_first
    w_mine = (w_index >= 0) & (w_index < w_owners)
    g_index = [y * g_row + f - wave[3] for wave in waves]
    g_mine = [(f >= wave[3]) & (f < wave[3] + g_row) & (y < g_owners // g_row) for wave in waves]

    def on_chip(step, c):
        other = lax.rem(chip + step, chips)
        return ((other // n_flux) * 2 + c, lax.rem(other, n_flux))

    pairs = (
        (std_hbm, std), (probes_hbm.at[0], probes.at[0]), (jac_hbm, jac),
        (probes_hbm.at[1], probes.at[1]), (weight_hbm, weight),
    )
    loads = [
        pltpu.make_async_copy(src, dst, load_sems.at[i]) for i, (src, dst) in enumerate(pairs)
    ]
    for load in loads:
        load.start()

    barrier = pltpu.get_barrier_semaphore()

    def signal(sem, device):
        pl.semaphore_signal(sem, inc=1, device_id=device, device_id_type=MESH)

    @pl.when(hub)
    def _():
        def greet(step):
            other = lax.rem(o * n_flux + f + step, n_obs * n_flux)
            signal(barrier, (other // n_flux, lax.rem(other, n_flux)))

        each(1, n_obs * n_flux, greet)

    @pl.when(jnp.logical_not(hub))
    def _():
        each(1, n_obs, lambda step: signal(barrier, (lax.rem(o + step, n_obs), f)))

    loads[0].wait()
    for s in range(flux_local // LANES):
        part = slice(s * LANES, (s + 1) * LANES)
        std_col[part, :] = column(std[:, part])

    def send(src, dst, number, device):
        copy = pltpu.make_async_remote_copy(
            src_ref=src, dst_ref=dst, send_sem=send_sems.at[number],
            recv_sem=recv_sems.at[number], device_id=device, device_id_type=MESH,
        )
        copy.start()
        return copy

    def forward(b):
        stacked = (probes[b].astype(F32) * std_col[...]).astype(BF16)
        partial = jnp.dot(jac[...], stacked, preferred_element_type=F32)
        fsend[b] = partial.reshape(w_owners, w_rows, half)

    def send_forward(b):
        for j in range(w_owners):
            pl.when(w_index != j)(
                lambda j=j: send(fsend.at[b, j], frecv.at[b, f], b, (o, w_first + j)) and None
            )

    loads[1].wait()
    loads[2].wait()
    forward(0)
    hubs = n_obs * h_count
    pl.when(hub)(lambda: pl.semaphore_wait(barrier, hubs - 1))
    pl.when(jnp.logical_not(hub))(lambda: pl.semaphore_wait(barrier, hubs + n_obs - 1))
    send_forward(0)
    loads[3].wait()
    forward(1)
    send_forward(1)

    @pl.when(jnp.logical_not(hub))
    def _():
        each(0, hubs, lambda step: signal(ready, (step % n_obs, h_first + step // n_obs)))

    loads[4].wait()
    for s in range(obs_local // LANES):
        part = slice(s * LANES, (s + 1) * LANES)
        weight_col[part, :] = column(weight[:, part])
    jt[...] = jac[...].T

    def send_jacobian(step):
        other = lax.rem(o + step, n_obs)
        rows = pl.ds(pl.multiple_of((other // 2) * chip_rows, chip_rows), chip_rows)
        send(jt.at[rows], jrecv.at[core * n_y + y], 2, (other, f))

    each(1, n_obs, send_jacobian)
    chip_at = pl.ds(pl.multiple_of(y * chip_rows, chip_rows), chip_rows)
    jrecv[core * n_y + y] = jt[chip_at, :]

    def weigh(b):
        frecv[b, f] = fsend[b, w_index]
        wait_bytes(frecv.at[b, pl.ds(0, n_flux - 1)], recv_sems.at[b])
        at = pl.ds(pl.multiple_of(w_index * w_rows, w_rows), w_rows)
        mine = y * w_owners + w_index
        wbuf[b, core, mine] = (jnp.sum(frecv[b], axis=0) * weight_col[at, :]).astype(BF16)
        own = wbuf.at[b, core, mine]
        each(1, chips, lambda step: send(own, own, 3 + b, on_chip(step, core)) and None)

    pl.when(hub)(lambda: pl.semaphore_wait(ready, n_obs * (n_flux - h_count)))

    @pl.when(w_mine)
    def _():
        weigh(0)
        weigh(1)

    def gathered(b):
        pl.when(w_mine)(
            lambda: wait_bytes(wbuf.at[b, core, pl.ds(0, n_y * w_owners - 1)], recv_sems.at[3 + b])
        )
        pl.when(jnp.logical_not(w_mine))(
            lambda: wait_bytes(wbuf.at[b, core], recv_sems.at[3 + b])
        )
        return send(wbuf.at[b, core], wbuf.at[b, core], 5 + b, partner)

    def adjoint(b, c):
        return jnp.dot(
            jnp.concatenate([jrecv[c * n_y + row] for row in range(n_y)], axis=1),
            wbuf[b, c].reshape(n_y * obs_local, half),
            preferred_element_type=F32,
        )

    def finish_sketch(b, own_half, across):
        across.wait_recv()
        sketch = (own_half + adjoint(b, 1 - core)) * std_col[chip_at, :]
        columns = slice(b * half, (b + 1) * half)

        @pl.when(core == 0)
        def _():
            sketch_out[:, columns] = sketch[:portion]

        @pl.when(core == 1)
        def _():
            sketch_out[:, columns] = sketch[portion:]

        return halves(sketch)

    def gram(left, right):
        return lax.dot_general(
            jnp.concatenate([left[0], left[0], left[1]], axis=0),
            jnp.concatenate([right[0], right[1], right[0]], axis=0),
            (((0,), (0,)), ((), ())), preferred_element_type=F32,
        )

    def pieces(block):
        return block.reshape(2, g_owners, TILE, half)

    def send_gram(number, start, count, first):
        at = pl.ds(start, count)
        for j in range(g_owners):
            owner = (2 * (j // g_row) + core, first + j % g_row)
            pl.when((f != owner[1]) | (y != j // g_row))(
                lambda j=j, owner=owner: send(
                    gsend.at[core, j, at], grecv.at[chip, at], number, owner
                ) and None
            )

    across0 = gathered(0)
    wait_bytes(jrecv.at[pl.ds(0, n_obs - 1)], recv_sems.at[2])
    own0 = adjoint(0, core)
    across1 = gathered(1)
    first = finish_sketch(0, own0, across0)
    gsend[:, :, 0] = pieces(gram(first, first))
    send_gram(*waves[0])
    own1 = adjoint(1, core)
    second = finish_sketch(1, own1, across1)
    both = [jnp.concatenate(pair, axis=1) for pair in zip(first, second)]
    trailing = gram(both, second)
    gsend[:, :, 1] = pieces(trailing[:half])
    gsend[:, :, 2] = pieces(trailing[half:])
    send_gram(*waves[1])

    work[:, half:] = identity(half)
    work_tail[:, half:] = identity(half)

    def total_gram(wave):
        number, start, count, _ = waves[wave]
        at = pl.ds(start, count)
        mine = core * g_owners + g_index[wave]
        grecv[chip, at] = gsend[core, g_index[wave], at]
        wait_bytes(grecv.at[pl.ds(0, chips - 1), at], recv_sems.at[number])
        gfull[mine, at] = jnp.sum(grecv[:, at], axis=0)

        def share(step):
            to = (step % n_obs, step // n_obs)
            own = gfull.at[mine, at]
            pl.when((o != to[0]) | (f != to[1]))(
                lambda: send(own, own, number + 2, to) and None
            )

        each(0, n_obs * n_flux, share)

    pl.when(g_mine[0])(lambda: total_gram(0))
    pl.when(g_mine[1])(lambda: total_gram(1))

    def arrived(wave):
        number, start, count, _ = waves[wave]
        at = pl.ds(start, count)

        @pl.when(g_mine[wave])
        def _():
            wait_bytes(gfull.at[pl.ds(0, 2 * g_owners - 1), at], recv_sems.at[number + 2])

        @pl.when(jnp.logical_not(g_mine[wave]))
        def _():
            wait_bytes(gfull.at[:, at], recv_sems.at[number + 2])

    arrived(0)
    work[:, :half] = gfull[:, 0].reshape(half, half)
    factor(work)
    arrived(1)
    inverse = work[:, half:]
    sketch = sketch_out[...]

    def product(a, b, dims):
        return lax.dot_general(
            a, b, (dims, ((), ())), precision=HIGHEST, preferred_element_type=F32
        )

    cross = product(inverse, gfull[:, 1].reshape(half, half), ((1,), (0,)))
    work_tail[:, :half] = gfull[:, 2].reshape(half, half) - product(cross, cross, ((0,), (0,)))
    first = product(sketch[:, :half], inverse, ((1,), (1,)))
    basis_out[:, :half] = first * scale
    basis_out[:, half:] = (sketch[:, half:] - product(first, cross, ((1,), (0,)))) * scale
    factor(work_tail)
    inverse_out[...] = work_tail[:, half:]

    each(1, n_obs, lambda step: wait_bytes(jrecv.at[0], send_sems.at[2]))
    for b, across in ((0, across0), (1, across1)):
        for j in range(w_owners):
            pl.when(w_index != j)(lambda b=b: wait_bytes(fsend.at[b, 0], send_sems.at[b]))
        pl.when(w_mine)(
            lambda b=b: each(
                1, chips, lambda step: wait_bytes(wbuf.at[b, core, 0], send_sems.at[3 + b])
            )
        )
        across.wait_send()
    for wave, (number, start, count, _) in enumerate(waves):
        piece = gfull.at[0, pl.ds(start, count)]
        each(0, g_owners - 1, lambda step: wait_bytes(piece, send_sems.at[number]))
        pl.when(jnp.logical_not(g_mine[wave]))(lambda: wait_bytes(piece, send_sems.at[number]))

        @pl.when(g_mine[wave])
        def _():
            each(1, 2 * chips, lambda step: wait_bytes(piece, send_sems.at[number + 2]))


def finish(sketch, basis, inverse, sketch_out, basis_out):
    half = inverse.shape[0]
    sketch_out[...] = sketch[...]
    basis_out[:, :half] = basis[:, :half]
    basis_out[:, half:] = lax.dot_general(
        basis[:, half:], inverse[...], (((1,), (1,)), ((), ())),
        precision=HIGHEST, preferred_element_type=F32,
    )


def body(jacobian, probes, prior_std, obs_weight):
    blocks, flux_local, probe_count = probes.shape
    obs_local = jacobian.shape[0]
    n_obs, n_flux = lax.axis_size("obs"), lax.axis_size("flux")
    width = blocks * probe_count
    half = width // 2
    portion = flux_local // n_obs
    n_y = n_obs // 2
    chips = n_y * n_flux
    w_rows = max(16, 2 * obs_local // n_flux)
    w_owners = obs_local // w_rows
    g_owners = half // 2 // TILE
    scale = math.sqrt(flux_local * n_flux)
    vmem = pl.BlockSpec(memory_space=pltpu.VMEM)
    out = jax.ShapeDtypeStruct((portion, width), F32)
    operands = (jacobian, probes, prior_std.reshape(1, -1), obs_weight.reshape(1, -1))
    sketch, basis, inverse = pl.pallas_call(
        functools.partial(kernel, (n_obs, n_flux), scale),
        out_shape=(out, out, jax.ShapeDtypeStruct((half, half), F32)),
        in_specs=[pl.BlockSpec(memory_space=pl.ANY)] * 4,
        out_specs=(vmem, vmem, vmem),
        scratch_shapes=[
            pltpu.VMEM(jacobian.shape, BF16),
            pltpu.VMEM(probes.shape, BF16),
            pltpu.VMEM((1, flux_local), F32),
            pltpu.VMEM((1, obs_local), F32),
            pltpu.SemaphoreType.DMA((5,)),
            pltpu.VMEM((flux_local, LANES), F32),
            pltpu.VMEM((obs_local, LANES), F32),
            pltpu.VMEM((flux_local, obs_local), BF16),
            pltpu.VMEM((n_obs, 2 * portion, obs_local), BF16),
            pltpu.VMEM((blocks, w_owners, w_rows, half), F32),
            pltpu.VMEM((blocks, n_flux, w_rows, half), F32),
            pltpu.VMEM((blocks, 2, n_y * w_owners, w_rows, half), BF16),
            pltpu.VMEM((2, g_owners, 3, TILE, half), F32),
            pltpu.VMEM((chips, 3, TILE, half), F32),
            pltpu.VMEM((2 * g_owners, 3, TILE, half), F32),
            pltpu.VMEM((half, width), F32),
            pltpu.VMEM((half, width), F32),
            pltpu.SemaphoreType.REGULAR,
            pltpu.SemaphoreType.DMA((11,)),
            pltpu.SemaphoreType.DMA((11,)),
        ],
        compiler_params=pltpu.CompilerParams(
            collective_id=0, has_side_effects=True, vmem_limit_bytes=24 << 20
        ),
    )(*[pltpu.with_memory_space_constraint(x, pltpu.HBM) for x in operands])
    return pl.pallas_call(
        finish,
        out_shape=(out, out),
        in_specs=[vmem] * 3,
        out_specs=(vmem, vmem),
        compiler_params=pltpu.CompilerParams(vmem_limit_bytes=8 << 20),
    )(sketch, basis, inverse)


def solution(mesh):
    in_specs = (P("obs", "flux"), P(None, "flux", None), P("flux"), P("obs"))
    out_specs = (P(("flux", "obs"), None), P(("flux", "obs"), None))
    return jax.shard_map(body, mesh=mesh, in_specs=in_specs, out_specs=out_specs, check_vma=False)
```

```python
import functools
import math

import jax
import jax.numpy as jnp
from jax import lax
from jax.experimental import pallas as pl
from jax.experimental.pallas import tpu as pltpu
from jax.sharding import PartitionSpec as P

MESH = pl.DeviceIdType.MESH
F32 = jnp.float32
BF16 = jnp.bfloat16
LANES = 128
PANEL = 64
TILE = 8


def each(lower, upper, step):
    if upper - lower <= 32:
        for value in range(lower, upper):
            step(value)
    else:
        lax.fori_loop(lower, upper, lambda value, carry: (step(value), carry)[1], 0)


def wait_bytes(ref, sem):
    pltpu.make_async_copy(ref, ref, sem).wait()


def column(row):
    return jnp.broadcast_to(row, (LANES, LANES)).T


def spread(x, k):
    return jnp.broadcast_to(x[k : k + 1, :], (TILE, LANES))


def lane(x, c):
    return jnp.broadcast_to(x[:, c : c + 1], (TILE, LANES))


def eliminate(rows, offset):
    index = lax.broadcasted_iota(jnp.int32, (TILE, LANES), 0)
    count = len(rows)
    cols = [lane(rows[0][0], offset + j) for j in range(TILE)]
    for t in range(count):
        base = offset + t * TILE
        lows = {b: [lane(rows[b][0], base + j) for j in range(TILE)] for b in range(t + 1, count)}
        ahead = [lane(rows[t + 1][0], base + TILE + j) for j in range(TILE)] if t + 1 < count else []
        diagonal = jnp.ones((TILE, LANES), F32)
        for k in range(TILE):
            pivot = spread(cols[k], k)
            diagonal = jnp.where(index == k, pivot, diagonal)
            inverse = 1.0 / pivot
            lead = [spread(part, k) for part in rows[t]]
            heads = [spread(col, k) if j > k else None for j, col in enumerate(cols)]
            if k < TILE - 1:
                multiplier = jnp.where(index > k, cols[k], 0.0) * inverse
                for j in range(k + 1, TILE):
                    cols[j] = cols[j] - multiplier * heads[j]
                rows[t] = [part - multiplier * row for part, row in zip(rows[t], lead)]
            for b, low in lows.items():
                multiplier = low[k] * inverse
                if b == t + 1:
                    ahead = [a - multiplier * spread(low[k], j) for j, a in enumerate(ahead)]
                for j in range(k + 1, TILE):
                    low[j] = low[j] - multiplier * heads[j]
                rows[b] = [part - multiplier * row for part, row in zip(rows[b], lead)]
        root = lax.rsqrt(diagonal)
        rows[t] = [part * root for part in rows[t]]
        cols = ahead
    return rows


def product(a, b, dims):
    def thirds(x):
        high = x.astype(BF16)
        rest = x - high.astype(F32)
        mid = rest.astype(BF16)
        return high, mid, (rest - mid.astype(F32)).astype(BF16)

    (a0, a1, a2), (b0, b1, b2) = thirds(a), thirds(b)
    return lax.dot_general(
        jnp.concatenate([a0, a0, a1, a1, a0, a2], axis=dims[0][0]),
        jnp.concatenate([b0, b1, b0, b1, b2, b0], axis=dims[1][0]),
        (dims, ((), ())), preferred_element_type=F32,
    )


def factor(work):
    size = work.shape[0]
    spans = [slice(s, s + LANES) for s in range(0, 2 * size, LANES)]
    for start in range(0, size, PANEL):
        if start:
            done = work[start - PANEL : start, :]
            update = product(done[:, :size], done, ((0,), (0,)))
            work[start:, :] = work[start:, :] - update[start:, :]
        rows = [
            [work[first : first + TILE, span] for span in spans]
            for first in range(start, start + PANEL, TILE)
        ]
        for t, row in enumerate(eliminate(rows, start)):
            first = start + t * TILE
            for span, part in zip(spans, row):
                work[first : first + TILE, span] = part


def identity(size):
    return (
        lax.broadcasted_iota(jnp.int32, (size, size), 0)
        == lax.broadcasted_iota(jnp.int32, (size, size), 1)
    ).astype(F32)


def halves(x):
    high = x.astype(BF16)
    return high, (x - high.astype(F32)).astype(BF16)


def kernel(
    sizes, scale, jac_hbm, probes_hbm, std_hbm, weight_hbm, sketch_out, basis_out, inverse_out,
    jac, probes, std, weight, load_sems, std_col, weight_col, jt, jrecv, fsend, frecv, wbuf,
    gsend, grecv, gfull, work, work_tail, ready, send_sems, recv_sems,
):
    n_obs, n_flux = sizes
    blocks, flux_local, probe_count = probes.shape
    obs_local = jac.shape[0]
    width = blocks * probe_count
    half = probe_count
    portion = flux_local // n_obs
    n_y = n_obs // 2
    chips = n_y * n_flux
    chip_rows = 2 * portion
    w_owners, w_rows = fsend.shape[1], fsend.shape[2]
    w_first = (n_flux - w_owners) // 2
    g_owners = gsend.shape[1]
    g_row = max(1, g_owners // n_y)
    center = (n_flux - g_row) // 2
    waves = ((7, 0, 1, max(center - 1, 0)), (8, 1, 2, center))
    h_first = min(w_first, waves[0][3], waves[1][3])
    h_count = max(w_first + w_owners, waves[0][3] + g_row, waves[1][3] + g_row) - h_first

    o, f = lax.axis_index("obs"), lax.axis_index("flux")
    core, y = lax.rem(o, 2), o // 2
    hub = (f >= h_first) & (f < h_first + h_count)
    chip = y * n_flux + f
    partner = (o + 1 - 2 * core, f)
    w_index = f - w_first
    w_mine = (w_index >= 0) & (w_index < w_owners)
    g_index = [y * g_row + f - wave[3] for wave in waves]
    g_mine = [(f >= wave[3]) & (f < wave[3] + g_row) & (y < g_owners // g_row) for wave in waves]

    def on_chip(step, c):
        other = lax.rem(chip + step, chips)
        return ((other // n_flux) * 2 + c, lax.rem(other, n_flux))

    pairs = (
        (std_hbm, std), (probes_hbm.at[0], probes.at[0]), (jac_hbm, jac),
        (probes_hbm.at[1], probes.at[1]), (weight_hbm, weight),
    )
    loads = [
        pltpu.make_async_copy(src, dst, load_sems.at[i]) for i, (src, dst) in enumerate(pairs)
    ]
    for load in loads:
        load.start()

    barrier = pltpu.get_barrier_semaphore()

    def signal(sem, device):
        pl.semaphore_signal(sem, inc=1, device_id=device, device_id_type=MESH)

    @pl.when(hub)
    def _():
        def greet(step):
            other = lax.rem(o * n_flux + f + step, n_obs * n_flux)
            signal(barrier, (other // n_flux, lax.rem(other, n_flux)))

        each(1, n_obs * n_flux, greet)

    @pl.when(jnp.logical_not(hub))
    def _():
        each(1, n_obs, lambda step: signal(barrier, (lax.rem(o + step, n_obs), f)))

    loads[0].wait()
    for s in range(flux_local // LANES):
        part = slice(s * LANES, (s + 1) * LANES)
        std_col[part, :] = column(std[:, part])

    def send(src, dst, number, device):
        copy = pltpu.make_async_remote_copy(
            src_ref=src, dst_ref=dst, send_sem=send_sems.at[number],
            recv_sem=recv_sems.at[number], device_id=device, device_id_type=MESH,
        )
        copy.start()
        return copy

    def forward(b):
        stacked = (probes[b].astype(F32) * std_col[...]).astype(BF16)
        partial = jnp.dot(jac[...], stacked, preferred_element_type=F32)
        fsend[b] = partial.reshape(w_owners, w_rows, half)

    def send_forward(b):
        for j in range(w_owners):
            pl.when(w_index != j)(
                lambda j=j: send(fsend.at[b, j], frecv.at[b, f], b, (o, w_first + j)) and None
            )

    loads[1].wait()
    loads[2].wait()
    forward(0)
    hubs = n_obs * h_count
    pl.when(hub)(lambda: pl.semaphore_wait(barrier, hubs - 1))
    pl.when(jnp.logical_not(hub))(lambda: pl.semaphore_wait(barrier, hubs + n_obs - 1))
    send_forward(0)
    loads[3].wait()
    forward(1)
    send_forward(1)

    @pl.when(jnp.logical_not(hub))
    def _():
        each(0, hubs, lambda step: signal(ready, (step % n_obs, h_first + step // n_obs)))

    loads[4].wait()
    for s in range(obs_local // LANES):
        part = slice(s * LANES, (s + 1) * LANES)
        weight_col[part, :] = column(weight[:, part])
    jt[...] = jac[...].T

    def send_jacobian(step):
        other = lax.rem(o + step, n_obs)
        rows = pl.ds(pl.multiple_of((other // 2) * chip_rows, chip_rows), chip_rows)
        send(jt.at[rows], jrecv.at[core * n_y + y], 2, (other, f))

    each(1, n_obs, send_jacobian)
    chip_at = pl.ds(pl.multiple_of(y * chip_rows, chip_rows), chip_rows)
    jrecv[core * n_y + y] = jt[chip_at, :]

    def weigh(b):
        frecv[b, f] = fsend[b, w_index]
        wait_bytes(frecv.at[b, pl.ds(0, n_flux - 1)], recv_sems.at[b])
        at = pl.ds(pl.multiple_of(w_index * w_rows, w_rows), w_rows)
        mine = y * w_owners + w_index
        wbuf[b, core, mine] = (jnp.sum(frecv[b], axis=0) * weight_col[at, :]).astype(BF16)
        own = wbuf.at[b, core, mine]
        each(1, chips, lambda step: send(own, own, 3 + b, on_chip(step, core)) and None)

    pl.when(hub)(lambda: pl.semaphore_wait(ready, n_obs * (n_flux - h_count)))

    @pl.when(w_mine)
    def _():
        weigh(0)
        weigh(1)

    def gathered(b):
        pl.when(w_mine)(
            lambda: wait_bytes(wbuf.at[b, core, pl.ds(0, n_y * w_owners - 1)], recv_sems.at[3 + b])
        )
        pl.when(jnp.logical_not(w_mine))(
            lambda: wait_bytes(wbuf.at[b, core], recv_sems.at[3 + b])
        )
        return send(wbuf.at[b, core], wbuf.at[b, core], 5 + b, partner)

    def adjoint(b, c):
        return jnp.dot(
            jnp.concatenate([jrecv[c * n_y + row] for row in range(n_y)], axis=1),
            wbuf[b, c].reshape(n_y * obs_local, half),
            preferred_element_type=F32,
        )

    def finish_sketch(b, own_half, across):
        across.wait_recv()
        sketch = (own_half + adjoint(b, 1 - core)) * std_col[chip_at, :]
        columns = slice(b * half, (b + 1) * half)

        @pl.when(core == 0)
        def _():
            sketch_out[:, columns] = sketch[:portion]

        @pl.when(core == 1)
        def _():
            sketch_out[:, columns] = sketch[portion:]

        return halves(sketch)

    def gram(left, right):
        return lax.dot_general(
            jnp.concatenate([left[0], left[0], left[1]], axis=0),
            jnp.concatenate([right[0], right[1], right[0]], axis=0),
            (((0,), (0,)), ((), ())), preferred_element_type=F32,
        )

    def pieces(block):
        return block.reshape(2, g_owners, TILE, half)

    def send_gram(number, start, count, first):
        at = pl.ds(start, count)
        for j in range(g_owners):
            owner = (2 * (j // g_row) + core, first + j % g_row)
            pl.when((f != owner[1]) | (y != j // g_row))(
                lambda j=j, owner=owner: send(
                    gsend.at[core, j, at], grecv.at[chip, at], number, owner
                ) and None
            )

    across0 = gathered(0)
    wait_bytes(jrecv.at[pl.ds(0, n_obs - 1)], recv_sems.at[2])
    own0 = adjoint(0, core)
    across1 = gathered(1)
    first = finish_sketch(0, own0, across0)
    gsend[:, :, 0] = pieces(gram(first, first))
    send_gram(*waves[0])
    own1 = adjoint(1, core)
    second = finish_sketch(1, own1, across1)
    both = [jnp.concatenate(pair, axis=1) for pair in zip(first, second)]
    trailing = gram(second, both)
    gsend[:, :, 1] = pieces(trailing[:, :half])
    gsend[:, :, 2] = pieces(trailing[:, half:])
    send_gram(*waves[1])

    work[:, half:] = identity(half)
    work_tail[:, half:] = identity(half)

    def total_gram(wave):
        number, start, count, _ = waves[wave]
        at = pl.ds(start, count)
        mine = core * g_owners + g_index[wave]
        grecv[chip, at] = gsend[core, g_index[wave], at]
        wait_bytes(grecv.at[pl.ds(0, chips - 1), at], recv_sems.at[number])
        gfull[mine, at] = jnp.sum(grecv[:, at], axis=0)

        def share(step):
            to = (step % n_obs, step // n_obs)
            own = gfull.at[mine, at]
            pl.when((o != to[0]) | (f != to[1]))(
                lambda: send(own, own, number + 2, to) and None
            )

        each(0, n_obs * n_flux, share)

    pl.when(g_mine[0])(lambda: total_gram(0))
    pl.when(g_mine[1])(lambda: total_gram(1))

    def arrived(wave):
        number, start, count, _ = waves[wave]
        at = pl.ds(start, count)

        @pl.when(g_mine[wave])
        def _():
            wait_bytes(gfull.at[pl.ds(0, 2 * g_owners - 1), at], recv_sems.at[number + 2])

        @pl.when(jnp.logical_not(g_mine[wave]))
        def _():
            wait_bytes(gfull.at[:, at], recv_sems.at[number + 2])

    arrived(0)
    work[:, :half] = gfull[:, 0].reshape(half, half)
    factor(work)
    arrived(1)
    inverse = work[:, half:]
    sketch = sketch_out[...]

    cross = product(gfull[:, 1].reshape(half, half), inverse, ((1,), (1,)))
    work_tail[:, :half] = gfull[:, 2].reshape(half, half) - product(cross, cross, ((1,), (1,)))
    first = product(sketch[:, :half], inverse, ((1,), (1,)))
    basis_out[:, :half] = first * scale
    basis_out[:, half:] = (sketch[:, half:] - product(first, cross, ((1,), (1,)))) * scale
    factor(work_tail)
    inverse_out[...] = work_tail[:, half:]

    each(1, n_obs, lambda step: wait_bytes(jrecv.at[0], send_sems.at[2]))
    for b, across in ((0, across0), (1, across1)):
        for j in range(w_owners):
            pl.when(w_index != j)(lambda b=b: wait_bytes(fsend.at[b, 0], send_sems.at[b]))
        pl.when(w_mine)(
            lambda b=b: each(
                1, chips, lambda step: wait_bytes(wbuf.at[b, core, 0], send_sems.at[3 + b])
            )
        )
        across.wait_send()
    for wave, (number, start, count, _) in enumerate(waves):
        piece = gfull.at[0, pl.ds(start, count)]
        each(0, g_owners - 1, lambda step: wait_bytes(piece, send_sems.at[number]))
        pl.when(jnp.logical_not(g_mine[wave]))(lambda: wait_bytes(piece, send_sems.at[number]))

        @pl.when(g_mine[wave])
        def _():
            each(1, 2 * chips, lambda step: wait_bytes(piece, send_sems.at[number + 2]))


def finish(sketch, basis, inverse, sketch_out, basis_out):
    half = inverse.shape[0]
    sketch_out[...] = sketch[...]
    basis_out[:, :half] = basis[:, :half]
    basis_out[:, half:] = product(basis[:, half:], inverse[...], ((1,), (1,)))


def body(jacobian, probes, prior_std, obs_weight):
    blocks, flux_local, probe_count = probes.shape
    obs_local = jacobian.shape[0]
    n_obs, n_flux = lax.axis_size("obs"), lax.axis_size("flux")
    width = blocks * probe_count
    half = width // 2
    portion = flux_local // n_obs
    n_y = n_obs // 2
    chips = n_y * n_flux
    w_rows = max(16, 2 * obs_local // n_flux)
    w_owners = obs_local // w_rows
    g_owners = half // 2 // TILE
    scale = math.sqrt(flux_local * n_flux)
    vmem = pl.BlockSpec(memory_space=pltpu.VMEM)
    out = jax.ShapeDtypeStruct((portion, width), F32)
    operands = (jacobian, probes, prior_std.reshape(1, -1), obs_weight.reshape(1, -1))
    sketch, basis, inverse = pl.pallas_call(
        functools.partial(kernel, (n_obs, n_flux), scale),
        out_shape=(out, out, jax.ShapeDtypeStruct((half, half), F32)),
        in_specs=[pl.BlockSpec(memory_space=pl.ANY)] * 4,
        out_specs=(vmem, vmem, vmem),
        scratch_shapes=[
            pltpu.VMEM(jacobian.shape, BF16),
            pltpu.VMEM(probes.shape, BF16),
            pltpu.VMEM((1, flux_local), F32),
            pltpu.VMEM((1, obs_local), F32),
            pltpu.SemaphoreType.DMA((5,)),
            pltpu.VMEM((flux_local, LANES), F32),
            pltpu.VMEM((obs_local, LANES), F32),
            pltpu.VMEM((flux_local, obs_local), BF16),
            pltpu.VMEM((n_obs, 2 * portion, obs_local), BF16),
            pltpu.VMEM((blocks, w_owners, w_rows, half), F32),
            pltpu.VMEM((blocks, n_flux, w_rows, half), F32),
            pltpu.VMEM((blocks, 2, n_y * w_owners, w_rows, half), BF16),
            pltpu.VMEM((2, g_owners, 3, TILE, half), F32),
            pltpu.VMEM((chips, 3, TILE, half), F32),
            pltpu.VMEM((2 * g_owners, 3, TILE, half), F32),
            pltpu.VMEM((half, width), F32),
            pltpu.VMEM((half, width), F32),
            pltpu.SemaphoreType.REGULAR,
            pltpu.SemaphoreType.DMA((11,)),
            pltpu.SemaphoreType.DMA((11,)),
        ],
        compiler_params=pltpu.CompilerParams(
            collective_id=0, has_side_effects=True, vmem_limit_bytes=24 << 20
        ),
    )(*[pltpu.with_memory_space_constraint(x, pltpu.HBM) for x in operands])
    return pl.pallas_call(
        finish,
        out_shape=(out, out),
        in_specs=[vmem] * 3,
        out_specs=(vmem, vmem),
        compiler_params=pltpu.CompilerParams(vmem_limit_bytes=8 << 20),
    )(sketch, basis, inverse)


def solution(mesh):
    in_specs = (P("obs", "flux"), P(None, "flux", None), P("flux"), P("obs"))
    out_specs = (P(("flux", "obs"), None), P(("flux", "obs"), None))
    return jax.shard_map(body, mesh=mesh, in_specs=in_specs, out_specs=out_specs, check_vma=False)
```

```python
import functools
import math

import jax
import jax.numpy as jnp
from jax import lax
from jax.experimental import pallas as pl
from jax.experimental.pallas import tpu as pltpu
from jax.sharding import PartitionSpec as P

MESH = pl.DeviceIdType.MESH
F32 = jnp.float32
BF16 = jnp.bfloat16
LANES = 128
PANEL = 64
TILE = 8


def each(lower, upper, step):
    if upper - lower <= 32:
        for value in range(lower, upper):
            step(value)
    else:
        lax.fori_loop(lower, upper, lambda value, carry: (step(value), carry)[1], 0)


def wait_bytes(ref, sem):
    pltpu.make_async_copy(ref, ref, sem).wait()


def column(row):
    return jnp.broadcast_to(row, (LANES, LANES)).T


def spread(x, k):
    return jnp.broadcast_to(x[k : k + 1, :], (TILE, LANES))


def lane(x, c):
    return jnp.broadcast_to(x[:, c : c + 1], (TILE, LANES))


def product(a, b, dims):
    def thirds(x):
        high = x.astype(BF16)
        rest = x - high.astype(F32)
        mid = rest.astype(BF16)
        return high, mid, (rest - mid.astype(F32)).astype(BF16)

    (a0, a1, a2), (b0, b1, b2) = thirds(a), thirds(b)
    return lax.dot_general(
        jnp.concatenate([a0, a0, a1, a1, a0, a2], axis=dims[0][0]),
        jnp.concatenate([b0, b1, b0, b1, b2, b0], axis=dims[1][0]),
        (dims, ((), ())), preferred_element_type=F32,
    )


def eliminate(rows, offset):
    index = lax.broadcasted_iota(jnp.int32, (TILE, LANES), 0)
    count = len(rows)
    cols = [lane(rows[0][0], offset + j) for j in range(TILE)]
    for t in range(count):
        base = offset + t * TILE
        lows = {b: [lane(rows[b][0], base + j) for j in range(TILE)] for b in range(t + 1, count)}
        ahead = [lane(rows[t + 1][0], base + TILE + j) for j in range(TILE)] if t + 1 < count else []
        diagonal = jnp.ones((TILE, LANES), F32)
        for k in range(TILE):
            pivot = spread(cols[k], k)
            diagonal = jnp.where(index == k, pivot, diagonal)
            inverse = 1.0 / pivot
            lead = [spread(part, k) for part in rows[t]]
            heads = [spread(col, k) if j > k else None for j, col in enumerate(cols)]
            if k < TILE - 1:
                multiplier = jnp.where(index > k, cols[k], 0.0) * inverse
                for j in range(k + 1, TILE):
                    cols[j] = cols[j] - multiplier * heads[j]
                rows[t] = [part - multiplier * row for part, row in zip(rows[t], lead)]
            for b, low in lows.items():
                multiplier = low[k] * inverse
                if b == t + 1:
                    ahead = [a - multiplier * spread(low[k], j) for j, a in enumerate(ahead)]
                for j in range(k + 1, TILE):
                    low[j] = low[j] - multiplier * heads[j]
                rows[b] = [part - multiplier * row for part, row in zip(rows[b], lead)]
        root = lax.rsqrt(diagonal)
        rows[t] = [part * root for part in rows[t]]
        cols = ahead
    return rows


def factor(block):
    size = block.shape[0]
    spans = [slice(s, s + LANES) for s in range(0, 2 * size, LANES)]
    rest = jnp.concatenate([block, identity(size)], axis=1)
    inverse = []
    for start in range(0, size, PANEL):
        rows = eliminate(
            [[rest[t : t + TILE, span] for span in spans] for t in range(0, PANEL, TILE)], start
        )
        done = jnp.concatenate([jnp.concatenate(row, axis=1) for row in rows], axis=0)
        inverse.append(done[:, size:])
        if start + PANEL < size:
            rest = rest[PANEL:] - product(done[:, :size], done, ((0,), (0,)))[start + PANEL :]
    return jnp.concatenate(inverse, axis=0)


def identity(size):
    return (
        lax.broadcasted_iota(jnp.int32, (size, size), 0)
        == lax.broadcasted_iota(jnp.int32, (size, size), 1)
    ).astype(F32)


def halves(x):
    high = x.astype(BF16)
    return high, (x - high.astype(F32)).astype(BF16)


def kernel(
    sizes, scale, jac_hbm, probes_hbm, std_hbm, weight_hbm, sketch_out, basis_out, inverse_out,
    jac, probes, std, weight, load_sems, std_col, weight_col, jt, jrecv, fsend, frecv, wbuf,
    gsend, grecv, gfull, work, ready, send_sems, recv_sems,
):
    n_obs, n_flux = sizes
    blocks, flux_local, probe_count = probes.shape
    obs_local = jac.shape[0]
    width = blocks * probe_count
    half = probe_count
    portion = flux_local // n_obs
    n_y = n_obs // 2
    chips = n_y * n_flux
    chip_rows = 2 * portion
    w_owners, w_rows = fsend.shape[1], fsend.shape[2]
    w_first = (n_flux - w_owners) // 2
    g_owners = gsend.shape[1]
    g_row = max(1, g_owners // n_y)
    center = (n_flux - g_row) // 2
    waves = ((7, 0, 1, max(center - 1, 0)), (8, 1, 2, center))
    h_first = min(w_first, waves[0][3], waves[1][3])
    h_count = max(w_first + w_owners, waves[0][3] + g_row, waves[1][3] + g_row) - h_first

    o, f = lax.axis_index("obs"), lax.axis_index("flux")
    core, y = lax.rem(o, 2), o // 2
    hub = (f >= h_first) & (f < h_first + h_count)
    chip = y * n_flux + f
    partner = (o + 1 - 2 * core, f)
    w_index = f - w_first
    w_mine = (w_index >= 0) & (w_index < w_owners)
    g_index = [y * g_row + f - wave[3] for wave in waves]
    g_mine = [(f >= wave[3]) & (f < wave[3] + g_row) & (y < g_owners // g_row) for wave in waves]

    def on_chip(step, c):
        other = lax.rem(chip + step, chips)
        return ((other // n_flux) * 2 + c, lax.rem(other, n_flux))

    pairs = (
        (std_hbm, std), (probes_hbm.at[0], probes.at[0]), (jac_hbm, jac),
        (probes_hbm.at[1], probes.at[1]), (weight_hbm, weight),
    )
    loads = [
        pltpu.make_async_copy(src, dst, load_sems.at[i]) for i, (src, dst) in enumerate(pairs)
    ]
    for load in loads:
        load.start()

    barrier = pltpu.get_barrier_semaphore()

    def signal(sem, device):
        pl.semaphore_signal(sem, inc=1, device_id=device, device_id_type=MESH)

    @pl.when(hub)
    def _():
        def greet(step):
            other = lax.rem(o * n_flux + f + step, n_obs * n_flux)
            signal(barrier, (other // n_flux, lax.rem(other, n_flux)))

        each(1, n_obs * n_flux, greet)

    @pl.when(jnp.logical_not(hub))
    def _():
        each(1, n_obs, lambda step: signal(barrier, (lax.rem(o + step, n_obs), f)))

    loads[0].wait()
    for s in range(flux_local // LANES):
        part = slice(s * LANES, (s + 1) * LANES)
        std_col[part, :] = column(std[:, part])

    def send(src, dst, number, device):
        copy = pltpu.make_async_remote_copy(
            src_ref=src, dst_ref=dst, send_sem=send_sems.at[number],
            recv_sem=recv_sems.at[number], device_id=device, device_id_type=MESH,
        )
        copy.start()
        return copy

    def forward(b):
        stacked = (probes[b].astype(F32) * std_col[...]).astype(BF16)
        partial = jnp.dot(jac[...], stacked, preferred_element_type=F32)
        fsend[b] = partial.reshape(w_owners, w_rows, half)

    def send_forward(b):
        for j in range(w_owners):
            pl.when(w_index != j)(
                lambda j=j: send(fsend.at[b, j], frecv.at[b, f], b, (o, w_first + j)) and None
            )

    loads[1].wait()
    loads[2].wait()
    forward(0)
    hubs = n_obs * h_count
    pl.when(hub)(lambda: pl.semaphore_wait(barrier, hubs - 1))
    pl.when(jnp.logical_not(hub))(lambda: pl.semaphore_wait(barrier, hubs + n_obs - 1))
    send_forward(0)
    loads[3].wait()
    forward(1)
    send_forward(1)

    @pl.when(jnp.logical_not(hub))
    def _():
        each(0, hubs, lambda step: signal(ready, (step % n_obs, h_first + step // n_obs)))

    loads[4].wait()
    for s in range(obs_local // LANES):
        part = slice(s * LANES, (s + 1) * LANES)
        weight_col[part, :] = column(weight[:, part])
    jt[...] = jac[...].T

    def send_jacobian(step):
        other = lax.rem(o + step, n_obs)
        rows = pl.ds(pl.multiple_of((other // 2) * chip_rows, chip_rows), chip_rows)
        send(jt.at[rows], jrecv.at[core * n_y + y], 2, (other, f))

    each(1, n_obs, send_jacobian)
    chip_at = pl.ds(pl.multiple_of(y * chip_rows, chip_rows), chip_rows)
    jrecv[core * n_y + y] = jt[chip_at, :]

    def weigh(b):
        frecv[b, f] = fsend[b, w_index]
        wait_bytes(frecv.at[b, pl.ds(0, n_flux - 1)], recv_sems.at[b])
        at = pl.ds(pl.multiple_of(w_index * w_rows, w_rows), w_rows)
        mine = y * w_owners + w_index
        wbuf[b, core, mine] = (jnp.sum(frecv[b], axis=0) * weight_col[at, :]).astype(BF16)
        own = wbuf.at[b, core, mine]
        each(1, chips, lambda step: send(own, own, 3 + b, on_chip(step, core)) and None)

    pl.when(hub)(lambda: pl.semaphore_wait(ready, n_obs * (n_flux - h_count)))

    @pl.when(w_mine)
    def _():
        weigh(0)
        weigh(1)

    def gathered(b):
        pl.when(w_mine)(
            lambda: wait_bytes(wbuf.at[b, core, pl.ds(0, n_y * w_owners - 1)], recv_sems.at[3 + b])
        )
        pl.when(jnp.logical_not(w_mine))(
            lambda: wait_bytes(wbuf.at[b, core], recv_sems.at[3 + b])
        )
        return send(wbuf.at[b, core], wbuf.at[b, core], 5 + b, partner)

    def adjoint(b, c):
        return jnp.dot(
            jnp.concatenate([jrecv[c * n_y + row] for row in range(n_y)], axis=1),
            wbuf[b, c].reshape(n_y * obs_local, half),
            preferred_element_type=F32,
        )

    def finish_sketch(b, own_half, across):
        across.wait_recv()
        return (own_half + adjoint(b, 1 - core)) * std_col[chip_at, :]

    def gram(left, right):
        return lax.dot_general(
            jnp.concatenate([left[0], left[0], left[1]], axis=0),
            jnp.concatenate([right[0], right[1], right[0]], axis=0),
            (((0,), (0,)), ((), ())), preferred_element_type=F32,
        )

    def pieces(block):
        return block.reshape(2, g_owners, TILE, half)

    def send_gram(number, start, count, first):
        at = pl.ds(start, count)
        for j in range(g_owners):
            owner = (2 * (j // g_row) + core, first + j % g_row)
            pl.when((f != owner[1]) | (y != j // g_row))(
                lambda j=j, owner=owner: send(
                    gsend.at[core, j, at], grecv.at[chip, at], number, owner
                ) and None
            )

    across0 = gathered(0)
    wait_bytes(jrecv.at[pl.ds(0, n_obs - 1)], recv_sems.at[2])
    own0 = adjoint(0, core)
    across1 = gathered(1)
    own1 = adjoint(1, core)
    sketch0 = finish_sketch(0, own0, across0)
    first = halves(sketch0)
    gsend[:, :, 0] = pieces(gram(first, first))
    send_gram(*waves[0])
    sketch1 = finish_sketch(1, own1, across1)
    second = halves(sketch1)
    both = [jnp.concatenate(pair, axis=1) for pair in zip(first, second)]
    trailing = gram(second, both)
    gsend[:, :, 1] = pieces(trailing[:, :half])
    gsend[:, :, 2] = pieces(trailing[:, half:])
    send_gram(*waves[1])

    for c in range(2):
        rows = slice(c * portion, (c + 1) * portion)

        @pl.when(core == c)
        def _():
            sketch_out[:, :half] = sketch0[rows]
            sketch_out[:, half:] = sketch1[rows]


    def total_gram(wave):
        number, start, count, _ = waves[wave]
        at = pl.ds(start, count)
        mine = core * g_owners + g_index[wave]
        grecv[chip, at] = gsend[core, g_index[wave], at]
        wait_bytes(grecv.at[pl.ds(0, chips - 1), at], recv_sems.at[number])
        gfull[mine, at] = jnp.sum(grecv[:, at], axis=0)

        def share(step):
            to = (step % n_obs, step // n_obs)
            own = gfull.at[mine, at]
            pl.when((o != to[0]) | (f != to[1]))(
                lambda: send(own, own, number + 2, to) and None
            )

        each(0, n_obs * n_flux, share)

    pl.when(g_mine[0])(lambda: total_gram(0))
    pl.when(g_mine[1])(lambda: total_gram(1))

    def arrived(wave):
        number, start, count, _ = waves[wave]
        at = pl.ds(start, count)

        @pl.when(g_mine[wave])
        def _():
            wait_bytes(gfull.at[pl.ds(0, 2 * g_owners - 1), at], recv_sems.at[number + 2])

        @pl.when(jnp.logical_not(g_mine[wave]))
        def _():
            wait_bytes(gfull.at[:, at], recv_sems.at[number + 2])

    each(1, n_obs, lambda step: wait_bytes(jrecv.at[0], send_sems.at[2]))
    for b, across in ((0, across0), (1, across1)):
        for j in range(w_owners):
            pl.when(w_index != j)(lambda b=b: wait_bytes(fsend.at[b, 0], send_sems.at[b]))
        pl.when(w_mine)(
            lambda b=b: each(
                1, chips, lambda step: wait_bytes(wbuf.at[b, core, 0], send_sems.at[3 + b])
            )
        )
        across.wait_send()
    for wave, (number, start, count, _) in enumerate(waves):
        piece = gfull.at[0, pl.ds(start, count)]
        each(0, g_owners - 1, lambda step: wait_bytes(piece, send_sems.at[number]))
        pl.when(jnp.logical_not(g_mine[wave]))(lambda: wait_bytes(piece, send_sems.at[number]))

    arrived(0)
    work[...] = factor(gfull[:, 0].reshape(half, half))
    arrived(1)
    for wave, (number, start, count, _) in enumerate(waves):
        piece = gfull.at[0, pl.ds(start, count)]

        @pl.when(g_mine[wave])
        def _():
            each(1, 2 * chips, lambda step: wait_bytes(piece, send_sems.at[number + 2]))

    inverse = work[...]
    sketch = sketch_out[...]

    cross = product(gfull[:, 1].reshape(half, half), inverse, ((1,), (1,)))
    rest = gfull[:, 2].reshape(half, half) - product(cross, cross, ((1,), (1,)))
    first = product(sketch[:, :half], inverse, ((1,), (1,)))
    basis_out[:, :half] = first * scale
    basis_out[:, half:] = (sketch[:, half:] - product(first, cross, ((1,), (1,)))) * scale
    inverse_out[...] = factor(rest)


def finish(sketch, basis, inverse, sketch_out, basis_out):
    half = inverse.shape[0]
    sketch_out[...] = sketch[...]
    basis_out[:, :half] = basis[:, :half]
    basis_out[:, half:] = product(basis[:, half:], inverse[...], ((1,), (1,)))


def body(jacobian, probes, prior_std, obs_weight):
    blocks, flux_local, probe_count = probes.shape
    obs_local = jacobian.shape[0]
    n_obs, n_flux = lax.axis_size("obs"), lax.axis_size("flux")
    width = blocks * probe_count
    half = width // 2
    portion = flux_local // n_obs
    n_y = n_obs // 2
    chips = n_y * n_flux
    w_rows = max(16, 2 * obs_local // n_flux)
    w_owners = obs_local // w_rows
    g_owners = half // 2 // TILE
    scale = math.sqrt(flux_local * n_flux)
    vmem = pl.BlockSpec(memory_space=pltpu.VMEM)
    out = jax.ShapeDtypeStruct((portion, width), F32)
    operands = (jacobian, probes, prior_std.reshape(1, -1), obs_weight.reshape(1, -1))
    sketch, basis, inverse = pl.pallas_call(
        functools.partial(kernel, (n_obs, n_flux), scale),
        out_shape=(out, out, jax.ShapeDtypeStruct((half, half), F32)),
        in_specs=[pl.BlockSpec(memory_space=pl.ANY)] * 4,
        out_specs=(vmem, vmem, vmem),
        scratch_shapes=[
            pltpu.VMEM(jacobian.shape, BF16),
            pltpu.VMEM(probes.shape, BF16),
            pltpu.VMEM((1, flux_local), F32),
            pltpu.VMEM((1, obs_local), F32),
            pltpu.SemaphoreType.DMA((5,)),
            pltpu.VMEM((flux_local, LANES), F32),
            pltpu.VMEM((obs_local, LANES), F32),
            pltpu.VMEM((flux_local, obs_local), BF16),
            pltpu.VMEM((n_obs, 2 * portion, obs_local), BF16),
            pltpu.VMEM((blocks, w_owners, w_rows, half), F32),
            pltpu.VMEM((blocks, n_flux, w_rows, half), F32),
            pltpu.VMEM((blocks, 2, n_y * w_owners, w_rows, half), BF16),
            pltpu.VMEM((2, g_owners, 3, TILE, half), F32),
            pltpu.VMEM((chips, 3, TILE, half), F32),
            pltpu.VMEM((2 * g_owners, 3, TILE, half), F32),
            pltpu.VMEM((half, half), F32),
            pltpu.SemaphoreType.REGULAR,
            pltpu.SemaphoreType.DMA((11,)),
            pltpu.SemaphoreType.DMA((11,)),
        ],
        compiler_params=pltpu.CompilerParams(
            collective_id=0, has_side_effects=True, vmem_limit_bytes=24 << 20
        ),
    )(*[pltpu.with_memory_space_constraint(x, pltpu.HBM) for x in operands])
    return pl.pallas_call(
        finish,
        out_shape=(out, out),
        in_specs=[vmem] * 3,
        out_specs=(vmem, vmem),
        compiler_params=pltpu.CompilerParams(vmem_limit_bytes=8 << 20),
    )(sketch, basis, inverse)


def solution(mesh):
    in_specs = (P("obs", "flux"), P(None, "flux", None), P("flux"), P("obs"))
    out_specs = (P(("flux", "obs"), None), P(("flux", "obs"), None))
    return jax.shard_map(body, mesh=mesh, in_specs=in_specs, out_specs=out_specs, check_vma=False)
```

```python
import functools
import math

import jax
import jax.numpy as jnp
from jax import lax
from jax.experimental import pallas as pl
from jax.experimental.pallas import tpu as pltpu
from jax.sharding import PartitionSpec as P

MESH = pl.DeviceIdType.MESH
F32 = jnp.float32
BF16 = jnp.bfloat16
LANES = 128
PANEL = 64
TILE = 8


def each(lower, upper, step):
    if upper - lower <= 32:
        for value in range(lower, upper):
            step(value)
    else:
        lax.fori_loop(lower, upper, lambda value, carry: (step(value), carry)[1], 0)


def wait_bytes(ref, sem):
    pltpu.make_async_copy(ref, ref, sem).wait()


def column(row):
    return jnp.broadcast_to(row, (LANES, LANES)).T


def spread(x, k):
    return jnp.broadcast_to(x[k : k + 1, :], (TILE, LANES))


def lane(x, c):
    return jnp.broadcast_to(x[:, c : c + 1], (TILE, LANES))


def product(a, b, dims):
    def thirds(x):
        high = x.astype(BF16)
        rest = x - high.astype(F32)
        mid = rest.astype(BF16)
        return high, mid, (rest - mid.astype(F32)).astype(BF16)

    (a0, a1, a2), (b0, b1, b2) = thirds(a), thirds(b)
    return lax.dot_general(
        jnp.concatenate([a0, a0, a1, a1, a0, a2], axis=dims[0][0]),
        jnp.concatenate([b0, b1, b0, b1, b2, b0], axis=dims[1][0]),
        (dims, ((), ())), preferred_element_type=F32,
    )


def eliminate(rows, offset):
    index = lax.broadcasted_iota(jnp.int32, (TILE, LANES), 0)
    count = len(rows)
    cols = [lane(rows[0][0], offset + j) for j in range(TILE)]
    for t in range(count):
        base = offset + t * TILE
        lows = {b: [lane(rows[b][0], base + j) for j in range(TILE)] for b in range(t + 1, count)}
        ahead = [lane(rows[t + 1][0], base + TILE + j) for j in range(TILE)] if t + 1 < count else []
        diagonal = jnp.ones((TILE, LANES), F32)
        for k in range(TILE):
            pivot = spread(cols[k], k)
            diagonal = jnp.where(index == k, pivot, diagonal)
            inverse = 1.0 / pivot
            lead = [spread(part, k) for part in rows[t]]
            heads = [spread(col, k) if j > k else None for j, col in enumerate(cols)]
            if k < TILE - 1:
                multiplier = jnp.where(index > k, cols[k], 0.0) * inverse
                for j in range(k + 1, TILE):
                    cols[j] = cols[j] - multiplier * heads[j]
                rows[t] = [part - multiplier * row for part, row in zip(rows[t], lead)]
            for b, low in lows.items():
                multiplier = low[k] * inverse
                if b == t + 1:
                    ahead = [a - multiplier * spread(low[k], j) for j, a in enumerate(ahead)]
                for j in range(k + 1, TILE):
                    low[j] = low[j] - multiplier * heads[j]
                rows[b] = [part - multiplier * row for part, row in zip(rows[b], lead)]
        root = lax.rsqrt(diagonal)
        rows[t] = [part * root for part in rows[t]]
        cols = ahead
    return rows


def factor(block):
    size = block.shape[0]
    spans = [slice(s, s + LANES) for s in range(0, 2 * size, LANES)]
    rest = jnp.concatenate([block, identity(size)], axis=1)
    inverse = []
    for start in range(0, size, PANEL):
        rows = eliminate(
            [[rest[t : t + TILE, span] for span in spans] for t in range(0, PANEL, TILE)], start
        )
        done = jnp.concatenate([jnp.concatenate(row, axis=1) for row in rows], axis=0)
        inverse.append(done[:, size:])
        if start + PANEL < size:
            rest = rest[PANEL:] - product(done[:, :size], done, ((0,), (0,)))[start + PANEL :]
    return jnp.concatenate(inverse, axis=0)


def identity(size):
    return (
        lax.broadcasted_iota(jnp.int32, (size, size), 0)
        == lax.broadcasted_iota(jnp.int32, (size, size), 1)
    ).astype(F32)


def halves(x):
    high = x.astype(BF16)
    return high, (x - high.astype(F32)).astype(BF16)


def kernel(
    sizes, scale, jac_hbm, probes_hbm, std_hbm, weight_hbm, sketch_out, basis_out, inverse_out,
    jac, probes, std, weight, load_sems, std_col, weight_col, jt, jrecv, fsend, frecv, wbuf,
    gsend, grecv, gfull, work, ready, send_sems, recv_sems,
):
    n_obs, n_flux = sizes
    blocks, flux_local, probe_count = probes.shape
    obs_local = jac.shape[0]
    width = blocks * probe_count
    half = probe_count
    portion = flux_local // n_obs
    n_y = n_obs // 2
    chips = n_y * n_flux
    chip_rows = 2 * portion
    w_owners, w_rows = fsend.shape[1], fsend.shape[2]
    w_first = (n_flux - w_owners) // 2
    w_total = n_y * w_owners
    g_owners = gsend.shape[1]
    g_row = max(1, g_owners // n_y)
    center = (n_flux - g_row) // 2
    waves = ((7, 0, 1, max(center - 1, 0)), (8, 1, 2, center))
    h_first = min(w_first, waves[0][3], waves[1][3])
    h_count = max(w_first + w_owners, waves[0][3] + g_row, waves[1][3] + g_row) - h_first

    o, f = lax.axis_index("obs"), lax.axis_index("flux")
    core, y = lax.rem(o, 2), o // 2
    hub = (f >= h_first) & (f < h_first + h_count)
    chip = y * n_flux + f
    partner = (o + 1 - 2 * core, f)
    w_index = f - w_first
    w_mine = (w_index >= 0) & (w_index < w_owners)
    g_index = [y * g_row + f - wave[3] for wave in waves]
    g_mine = [(f >= wave[3]) & (f < wave[3] + g_row) & (y < g_owners // g_row) for wave in waves]

    def on_chip(step, c):
        other = lax.rem(chip + step, chips)
        return ((other // n_flux) * 2 + c, lax.rem(other, n_flux))

    pairs = (
        (std_hbm, std), (probes_hbm.at[0], probes.at[0]), (jac_hbm, jac),
        (probes_hbm.at[1], probes.at[1]), (weight_hbm, weight),
    )
    loads = [
        pltpu.make_async_copy(src, dst, load_sems.at[i]) for i, (src, dst) in enumerate(pairs)
    ]
    for load in loads:
        load.start()

    barrier = pltpu.get_barrier_semaphore()

    def signal(sem, device):
        pl.semaphore_signal(sem, inc=1, device_id=device, device_id_type=MESH)

    @pl.when(hub)
    def _():
        def greet(step):
            other = lax.rem(o * n_flux + f + step, n_obs * n_flux)
            signal(barrier, (other // n_flux, lax.rem(other, n_flux)))

        each(1, n_obs * n_flux, greet)

    @pl.when(jnp.logical_not(hub))
    def _():
        each(1, n_obs, lambda step: signal(barrier, (lax.rem(o + step, n_obs), f)))

    loads[0].wait()
    for s in range(flux_local // LANES):
        part = slice(s * LANES, (s + 1) * LANES)
        std_col[part, :] = column(std[:, part])

    def send(src, dst, number, device):
        copy = pltpu.make_async_remote_copy(
            src_ref=src, dst_ref=dst, send_sem=send_sems.at[number],
            recv_sem=recv_sems.at[number], device_id=device, device_id_type=MESH,
        )
        copy.start()
        return copy

    def forward(b):
        stacked = (probes[b].astype(F32) * std_col[...]).astype(BF16)
        partial = jnp.dot(jac[...], stacked, preferred_element_type=F32)
        fsend[b] = partial.reshape(w_owners, w_rows, half)

    def send_forward(b):
        for j in range(w_owners):
            pl.when(w_index != j)(
                lambda j=j: send(fsend.at[b, j], frecv.at[b, f], b, (o, w_first + j)) and None
            )

    loads[1].wait()
    loads[2].wait()
    forward(0)
    hubs = n_obs * h_count
    pl.when(hub)(lambda: pl.semaphore_wait(barrier, hubs - 1))
    pl.when(jnp.logical_not(hub))(lambda: pl.semaphore_wait(barrier, hubs + n_obs - 1))
    send_forward(0)
    loads[3].wait()
    forward(1)
    send_forward(1)

    @pl.when(jnp.logical_not(hub))
    def _():
        each(0, hubs, lambda step: signal(ready, (step % n_obs, h_first + step // n_obs)))

    loads[4].wait()
    for s in range(obs_local // LANES):
        part = slice(s * LANES, (s + 1) * LANES)
        weight_col[part, :] = column(weight[:, part])
    jt[...] = jac[...].T

    def send_jacobian(step):
        other = lax.rem(o + step, n_obs)
        rows = pl.ds(pl.multiple_of((other // 2) * chip_rows, chip_rows), chip_rows)
        send(jt.at[rows], jrecv.at[core * n_y + y], 2, (other, f))

    each(1, n_obs, send_jacobian)
    chip_at = pl.ds(pl.multiple_of(y * chip_rows, chip_rows), chip_rows)
    jrecv[core * n_y + y] = jt[chip_at, :]

    def weigh(b):
        frecv[b, f] = fsend[b, w_index]
        wait_bytes(frecv.at[b, pl.ds(0, n_flux - 1)], recv_sems.at[b])
        at = pl.ds(pl.multiple_of(w_index * w_rows, w_rows), w_rows)
        mine = core * w_total + y * w_owners + w_index
        wbuf[b, mine] = (jnp.sum(frecv[b], axis=0) * weight_col[at, :]).astype(BF16)
        own = wbuf.at[b, mine]

        def share(step, c):
            send(own, own, 3 + b, on_chip(step, c))

        each(1, chips, lambda step: share(step, core))
        if b == 1:
            each(0, chips, lambda step: share(step, 1 - core))

    pl.when(hub)(lambda: pl.semaphore_wait(ready, n_obs * (n_flux - h_count)))

    @pl.when(w_mine)
    def _():
        weigh(0)
        weigh(1)

    def gathered(b):
        count = w_total * (1 + b)
        pl.when(w_mine)(lambda: wait_bytes(wbuf.at[b, pl.ds(0, count - 1)], recv_sems.at[3 + b]))
        pl.when(jnp.logical_not(w_mine))(
            lambda: wait_bytes(wbuf.at[b, pl.ds(0, count)], recv_sems.at[3 + b])
        )

    def adjoint(b, c):
        return jnp.dot(
            jnp.concatenate([jrecv[c * n_y + row] for row in range(n_y)], axis=1),
            wbuf[b, pl.ds(c * w_total, w_total)].reshape(n_y * obs_local, half),
            preferred_element_type=F32,
        )

    def gram(left, right):
        return lax.dot_general(
            jnp.concatenate([left[0], left[0], left[1]], axis=0),
            jnp.concatenate([right[0], right[1], right[0]], axis=0),
            (((0,), (0,)), ((), ())), preferred_element_type=F32,
        )

    def pieces(block):
        return block.reshape(2, g_owners, TILE, half)

    def send_gram(number, start, count, first):
        at = pl.ds(start, count)
        for j in range(g_owners):
            owner = (2 * (j // g_row) + core, first + j % g_row)
            pl.when((f != owner[1]) | (y != j // g_row))(
                lambda j=j, owner=owner: send(
                    gsend.at[core, j, at], grecv.at[chip, at], number, owner
                ) and None
            )

    gathered(0)
    half_at = pl.ds(core * w_total, w_total)
    across = send(wbuf.at[0, half_at], wbuf.at[0, half_at], 5, partner)
    wait_bytes(jrecv.at[pl.ds(0, n_obs - 1)], recv_sems.at[2])
    own_half = adjoint(0, core)
    across.wait_recv()
    sketch0 = (own_half + adjoint(0, 1 - core)) * std_col[chip_at, :]
    first = halves(sketch0)
    gsend[:, :, 0] = pieces(gram(first, first))
    send_gram(*waves[0])
    gathered(1)
    sketch1 = (adjoint(1, 0) + adjoint(1, 1)) * std_col[chip_at, :]
    second = halves(sketch1)
    both = [jnp.concatenate(pair, axis=1) for pair in zip(first, second)]
    trailing = gram(second, both)
    gsend[:, :, 1] = pieces(trailing[:, :half])
    gsend[:, :, 2] = pieces(trailing[:, half:])
    send_gram(*waves[1])

    for c in range(2):
        rows = slice(c * portion, (c + 1) * portion)

        @pl.when(core == c)
        def _():
            sketch_out[:, :half] = sketch0[rows]
            sketch_out[:, half:] = sketch1[rows]


    def total_gram(wave):
        number, start, count, _ = waves[wave]
        at = pl.ds(start, count)
        mine = core * g_owners + g_index[wave]
        grecv[chip, at] = gsend[core, g_index[wave], at]
        wait_bytes(grecv.at[pl.ds(0, chips - 1), at], recv_sems.at[number])
        gfull[mine, at] = jnp.sum(grecv[:, at], axis=0)

        def share(step):
            to = (step % n_obs, step // n_obs)
            own = gfull.at[mine, at]
            pl.when((o != to[0]) | (f != to[1]))(
                lambda: send(own, own, number + 2, to) and None
            )

        each(0, n_obs * n_flux, share)

    pl.when(g_mine[0])(lambda: total_gram(0))
    pl.when(g_mine[1])(lambda: total_gram(1))

    def arrived(wave):
        number, start, count, _ = waves[wave]
        at = pl.ds(start, count)

        @pl.when(g_mine[wave])
        def _():
            wait_bytes(gfull.at[pl.ds(0, 2 * g_owners - 1), at], recv_sems.at[number + 2])

        @pl.when(jnp.logical_not(g_mine[wave]))
        def _():
            wait_bytes(gfull.at[:, at], recv_sems.at[number + 2])

    each(1, n_obs, lambda step: wait_bytes(jrecv.at[0], send_sems.at[2]))
    for b in range(blocks):
        for j in range(w_owners):
            pl.when(w_index != j)(lambda b=b: wait_bytes(fsend.at[b, 0], send_sems.at[b]))
        pl.when(w_mine)(
            lambda b=b: each(
                1, chips * (1 + b), lambda step: wait_bytes(wbuf.at[b, 0], send_sems.at[3 + b])
            )
        )
    across.wait_send()
    for wave, (number, start, count, _) in enumerate(waves):
        piece = gfull.at[0, pl.ds(start, count)]
        each(0, g_owners - 1, lambda step: wait_bytes(piece, send_sems.at[number]))
        pl.when(jnp.logical_not(g_mine[wave]))(lambda: wait_bytes(piece, send_sems.at[number]))

    arrived(0)
    work[...] = factor(gfull[:, 0].reshape(half, half))
    arrived(1)
    for wave, (number, start, count, _) in enumerate(waves):
        piece = gfull.at[0, pl.ds(start, count)]

        @pl.when(g_mine[wave])
        def _():
            each(1, 2 * chips, lambda step: wait_bytes(piece, send_sems.at[number + 2]))

    inverse = work[...]
    sketch = sketch_out[...]

    cross = product(gfull[:, 1].reshape(half, half), inverse, ((1,), (1,)))
    rest = gfull[:, 2].reshape(half, half) - product(cross, cross, ((1,), (1,)))
    first = product(sketch[:, :half], inverse, ((1,), (1,)))
    basis_out[:, :half] = first * scale
    basis_out[:, half:] = (sketch[:, half:] - product(first, cross, ((1,), (1,)))) * scale
    inverse_out[...] = factor(rest)


def finish(sketch, basis, inverse, sketch_out, basis_out):
    half = inverse.shape[0]
    sketch_out[...] = sketch[...]
    basis_out[:, :half] = basis[:, :half]
    basis_out[:, half:] = product(basis[:, half:], inverse[...], ((1,), (1,)))


def body(jacobian, probes, prior_std, obs_weight):
    blocks, flux_local, probe_count = probes.shape
    obs_local = jacobian.shape[0]
    n_obs, n_flux = lax.axis_size("obs"), lax.axis_size("flux")
    width = blocks * probe_count
    half = width // 2
    portion = flux_local // n_obs
    n_y = n_obs // 2
    chips = n_y * n_flux
    w_rows = max(16, 2 * obs_local // n_flux)
    w_owners = obs_local // w_rows
    g_owners = half // 2 // TILE
    scale = math.sqrt(flux_local * n_flux)
    vmem = pl.BlockSpec(memory_space=pltpu.VMEM)
    out = jax.ShapeDtypeStruct((portion, width), F32)
    operands = (jacobian, probes, prior_std.reshape(1, -1), obs_weight.reshape(1, -1))
    sketch, basis, inverse = pl.pallas_call(
        functools.partial(kernel, (n_obs, n_flux), scale),
        out_shape=(out, out, jax.ShapeDtypeStruct((half, half), F32)),
        in_specs=[pl.BlockSpec(memory_space=pl.ANY)] * 4,
        out_specs=(vmem, vmem, vmem),
        scratch_shapes=[
            pltpu.VMEM(jacobian.shape, BF16),
            pltpu.VMEM(probes.shape, BF16),
            pltpu.VMEM((1, flux_local), F32),
            pltpu.VMEM((1, obs_local), F32),
            pltpu.SemaphoreType.DMA((5,)),
            pltpu.VMEM((flux_local, LANES), F32),
            pltpu.VMEM((obs_local, LANES), F32),
            pltpu.VMEM((flux_local, obs_local), BF16),
            pltpu.VMEM((n_obs, 2 * portion, obs_local), BF16),
            pltpu.VMEM((blocks, w_owners, w_rows, half), F32),
            pltpu.VMEM((blocks, n_flux, w_rows, half), F32),
            pltpu.VMEM((blocks, 2 * n_y * w_owners, w_rows, half), BF16),
            pltpu.VMEM((2, g_owners, 3, TILE, half), F32),
            pltpu.VMEM((chips, 3, TILE, half), F32),
            pltpu.VMEM((2 * g_owners, 3, TILE, half), F32),
            pltpu.VMEM((half, half), F32),
            pltpu.SemaphoreType.REGULAR,
            pltpu.SemaphoreType.DMA((11,)),
            pltpu.SemaphoreType.DMA((11,)),
        ],
        compiler_params=pltpu.CompilerParams(
            collective_id=0, has_side_effects=True, vmem_limit_bytes=24 << 20
        ),
    )(*[pltpu.with_memory_space_constraint(x, pltpu.HBM) for x in operands])
    return pl.pallas_call(
        finish,
        out_shape=(out, out),
        in_specs=[vmem] * 3,
        out_specs=(vmem, vmem),
        compiler_params=pltpu.CompilerParams(vmem_limit_bytes=8 << 20),
    )(sketch, basis, inverse)


def solution(mesh):
    in_specs = (P("obs", "flux"), P(None, "flux", None), P("flux"), P("obs"))
    out_specs = (P(("flux", "obs"), None), P(("flux", "obs"), None))
    return jax.shard_map(body, mesh=mesh, in_specs=in_specs, out_specs=out_specs, check_vma=False)
```

```python
import functools
import math

import jax
import jax.numpy as jnp
from jax import lax
from jax.experimental import pallas as pl
from jax.experimental.pallas import tpu as pltpu
from jax.sharding import PartitionSpec as P

MESH = pl.DeviceIdType.MESH
F32 = jnp.float32
BF16 = jnp.bfloat16
LANES = 128
PANEL = 64
TILE = 8


def each(lower, upper, step):
    if upper - lower <= 32:
        for value in range(lower, upper):
            step(value)
    else:
        lax.fori_loop(lower, upper, lambda value, carry: (step(value), carry)[1], 0)


def wait_bytes(ref, sem):
    pltpu.make_async_copy(ref, ref, sem).wait()


def column(row):
    return jnp.broadcast_to(row, (LANES, LANES)).T


def spread(x, k):
    return jnp.broadcast_to(x[k : k + 1, :], (TILE, LANES))


def lane(x, c):
    return jnp.broadcast_to(x[:, c : c + 1], (TILE, LANES))


def product(a, b, dims):
    def thirds(x):
        high = x.astype(BF16)
        rest = x - high.astype(F32)
        mid = rest.astype(BF16)
        return high, mid, (rest - mid.astype(F32)).astype(BF16)

    (a0, a1, a2), (b0, b1, b2) = thirds(a), thirds(b)
    return lax.dot_general(
        jnp.concatenate([a0, a0, a1, a1, a0, a2], axis=dims[0][0]),
        jnp.concatenate([b0, b1, b0, b1, b2, b0], axis=dims[1][0]),
        (dims, ((), ())), preferred_element_type=F32,
    )


def eliminate(rows, offset):
    index = lax.broadcasted_iota(jnp.int32, (TILE, LANES), 0)
    count = len(rows)
    cols = [lane(rows[0][0], offset + j) for j in range(TILE)]
    for t in range(count):
        base = offset + t * TILE
        lows = {b: [lane(rows[b][0], base + j) for j in range(TILE)] for b in range(t + 1, count)}
        ahead = [lane(rows[t + 1][0], base + TILE + j) for j in range(TILE)] if t + 1 < count else []
        diagonal = jnp.ones((TILE, LANES), F32)
        for k in range(TILE):
            pivot = spread(cols[k], k)
            diagonal = jnp.where(index == k, pivot, diagonal)
            inverse = 1.0 / pivot
            lead = [spread(part, k) for part in rows[t]]
            heads = [spread(col, k) if j > k else None for j, col in enumerate(cols)]
            if k < TILE - 1:
                multiplier = jnp.where(index > k, cols[k], 0.0) * inverse
                for j in range(k + 1, TILE):
                    cols[j] = cols[j] - multiplier * heads[j]
                rows[t] = [part - multiplier * row for part, row in zip(rows[t], lead)]
            for b, low in lows.items():
                multiplier = low[k] * inverse
                if b == t + 1:
                    ahead = [a - multiplier * spread(low[k], j) for j, a in enumerate(ahead)]
                for j in range(k + 1, TILE):
                    low[j] = low[j] - multiplier * heads[j]
                rows[b] = [part - multiplier * row for part, row in zip(rows[b], lead)]
        root = lax.rsqrt(diagonal)
        rows[t] = [part * root for part in rows[t]]
        cols = ahead
    return rows


def factor(block):
    size = block.shape[0]
    spans = [slice(s, s + LANES) for s in range(0, 2 * size, LANES)]
    rest = jnp.concatenate([block, identity(size)], axis=1)
    inverse = []
    for start in range(0, size, PANEL):
        rows = eliminate(
            [[rest[t : t + TILE, span] for span in spans] for t in range(0, PANEL, TILE)], start
        )
        done = jnp.concatenate([jnp.concatenate(row, axis=1) for row in rows], axis=0)
        inverse.append(done[:, size:])
        if start + PANEL < size:
            rest = rest[PANEL:] - product(done[:, :size], done, ((0,), (0,)))[start + PANEL :]
    return jnp.concatenate(inverse, axis=0)


def identity(size):
    return (
        lax.broadcasted_iota(jnp.int32, (size, size), 0)
        == lax.broadcasted_iota(jnp.int32, (size, size), 1)
    ).astype(F32)


def halves(x):
    high = x.astype(BF16)
    return high, (x - high.astype(F32)).astype(BF16)


def kernel(
    sizes, scale, jac_hbm, probes_hbm, std_hbm, weight_hbm, sketch_out, basis_out, inverse_out,
    jac, probes, std, weight, load_sems, std_col, weight_col, jt, jrecv, fsend, frecv, wbuf,
    gsend, grecv, gfull, work, ready, send_sems, recv_sems,
):
    n_obs, n_flux = sizes
    blocks, flux_local, probe_count = probes.shape
    obs_local = jac.shape[0]
    width = blocks * probe_count
    half = probe_count
    portion = flux_local // n_obs
    n_y = n_obs // 2
    chips = n_y * n_flux
    chip_rows = 2 * portion
    w_owners, w_rows = fsend.shape[1], fsend.shape[2]
    w_first = (n_flux - w_owners) // 2
    w_total = n_y * w_owners
    g_owners = gsend.shape[1]
    g_row = max(1, g_owners // n_y)
    center = (n_flux - g_row) // 2
    waves = ((7, 0, 1, max(center - 1, 0)), (8, 1, 2, center))
    h_first = min(w_first, waves[0][3], waves[1][3])
    h_count = max(w_first + w_owners, waves[0][3] + g_row, waves[1][3] + g_row) - h_first

    o, f = lax.axis_index("obs"), lax.axis_index("flux")
    core, y = lax.rem(o, 2), o // 2
    hub = (f >= h_first) & (f < h_first + h_count)
    chip = y * n_flux + f
    partner = (o + 1 - 2 * core, f)
    w_index = f - w_first
    w_mine = (w_index >= 0) & (w_index < w_owners)
    g_index = [y * g_row + f - wave[3] for wave in waves]
    g_mine = [(f >= wave[3]) & (f < wave[3] + g_row) & (y < g_owners // g_row) for wave in waves]

    def on_chip(step, c):
        other = lax.rem(chip + step, chips)
        return ((other // n_flux) * 2 + c, lax.rem(other, n_flux))

    pairs = (
        (std_hbm, std), (probes_hbm.at[0], probes.at[0]), (jac_hbm, jac),
        (probes_hbm.at[1], probes.at[1]), (weight_hbm, weight),
    )
    loads = [
        pltpu.make_async_copy(src, dst, load_sems.at[i]) for i, (src, dst) in enumerate(pairs)
    ]
    for load in loads:
        load.start()

    barrier = pltpu.get_barrier_semaphore()

    def signal(sem, device):
        pl.semaphore_signal(sem, inc=1, device_id=device, device_id_type=MESH)

    @pl.when(hub)
    def _():
        def greet(step):
            other = lax.rem(o * n_flux + f + step, n_obs * n_flux)
            signal(barrier, (other // n_flux, lax.rem(other, n_flux)))

        each(1, n_obs * n_flux, greet)

    @pl.when(jnp.logical_not(hub))
    def _():
        each(1, n_obs, lambda step: signal(barrier, (lax.rem(o + step, n_obs), f)))

    loads[0].wait()
    for s in range(flux_local // LANES):
        part = slice(s * LANES, (s + 1) * LANES)
        std_col[part, :] = column(std[:, part])

    def send(src, dst, number, device):
        copy = pltpu.make_async_remote_copy(
            src_ref=src, dst_ref=dst, send_sem=send_sems.at[number],
            recv_sem=recv_sems.at[number], device_id=device, device_id_type=MESH,
        )
        copy.start()
        return copy

    def forward(b):
        stacked = (probes[b].astype(F32) * std_col[...]).astype(BF16)
        partial = jnp.dot(jac[...], stacked, preferred_element_type=F32)
        fsend[b] = partial.reshape(w_owners, w_rows, half)

    def send_forward(b):
        for j in range(w_owners):
            pl.when(w_index != j)(
                lambda j=j: send(fsend.at[b, j], frecv.at[b, f], b, (o, w_first + j)) and None
            )

    loads[1].wait()
    loads[2].wait()
    forward(0)
    hubs = n_obs * h_count
    pl.when(hub)(lambda: pl.semaphore_wait(barrier, hubs - 1))
    pl.when(jnp.logical_not(hub))(lambda: pl.semaphore_wait(barrier, hubs + n_obs - 1))
    send_forward(0)
    loads[3].wait()
    forward(1)
    send_forward(1)

    @pl.when(jnp.logical_not(hub))
    def _():
        each(0, hubs, lambda step: signal(ready, (step % n_obs, h_first + step // n_obs)))

    loads[4].wait()
    for s in range(obs_local // LANES):
        part = slice(s * LANES, (s + 1) * LANES)
        weight_col[part, :] = column(weight[:, part])
    jt[...] = jac[...].T

    def send_jacobian(step):
        other = lax.rem(o + step, n_obs)
        rows = pl.ds(pl.multiple_of((other // 2) * chip_rows, chip_rows), chip_rows)
        send(jt.at[rows], jrecv.at[core * n_y + y], 2, (other, f))

    each(1, n_obs, send_jacobian)
    chip_at = pl.ds(pl.multiple_of(y * chip_rows, chip_rows), chip_rows)
    jrecv[core * n_y + y] = jt[chip_at, :]

    def weigh(b):
        frecv[b, f] = fsend[b, w_index]
        wait_bytes(frecv.at[b, pl.ds(0, n_flux - 1)], recv_sems.at[b])
        at = pl.ds(pl.multiple_of(w_index * w_rows, w_rows), w_rows)
        mine = core * w_total + y * w_owners + w_index
        wbuf[b, mine] = (jnp.sum(frecv[b], axis=0) * weight_col[at, :]).astype(BF16)
        own = wbuf.at[b, mine]

        def share(step, c):
            send(own, own, 3 + b, on_chip(step, c))

        each(1, chips, lambda step: share(step, core))
        if b == 1:
            each(0, chips, lambda step: share(step, 1 - core))

    pl.when(hub)(lambda: pl.semaphore_wait(ready, n_obs * (n_flux - h_count)))

    @pl.when(w_mine)
    def _():
        weigh(0)
        weigh(1)

    def gathered(b):
        count = w_total * (1 + b)
        pl.when(w_mine)(lambda: wait_bytes(wbuf.at[b, pl.ds(0, count - 1)], recv_sems.at[3 + b]))
        pl.when(jnp.logical_not(w_mine))(
            lambda: wait_bytes(wbuf.at[b, pl.ds(0, count)], recv_sems.at[3 + b])
        )

    def adjoint(b, c):
        return jnp.dot(
            jnp.concatenate([jrecv[c * n_y + row] for row in range(n_y)], axis=1),
            wbuf[b, pl.ds(c * w_total, w_total)].reshape(n_y * obs_local, half),
            preferred_element_type=F32,
        )

    def gram(left, right):
        return lax.dot_general(
            jnp.concatenate([left[0], left[0], left[1]], axis=0),
            jnp.concatenate([right[0], right[1], right[0]], axis=0),
            (((0,), (0,)), ((), ())), preferred_element_type=F32,
        )

    def pieces(block):
        return block.reshape(2, g_owners, TILE, half)

    def send_gram(number, start, count, first):
        at = pl.ds(start, count)
        for j in range(g_owners):
            owner = (2 * (j // g_row) + core, first + j % g_row)
            pl.when((f != owner[1]) | (y != j // g_row))(
                lambda j=j, owner=owner: send(
                    gsend.at[core, j, at], grecv.at[chip, at], number, owner
                ) and None
            )

    gathered(0)
    half_at = pl.ds(core * w_total, w_total)
    across = send(wbuf.at[0, half_at], wbuf.at[0, half_at], 5, partner)
    wait_bytes(jrecv.at[pl.ds(0, n_obs - 1)], recv_sems.at[2])
    own_half = adjoint(0, core)
    across.wait_recv()
    sketch0 = (own_half + adjoint(0, 1 - core)) * std_col[chip_at, :]
    first = halves(sketch0)
    gsend[:, :, 0] = pieces(gram(first, first))
    send_gram(*waves[0])
    gathered(1)
    columns = jnp.concatenate([jrecv[row] for row in range(n_obs)], axis=1)
    rows = wbuf[1].reshape(n_obs * obs_local, half)
    sketch1 = jnp.dot(columns, rows, preferred_element_type=F32) * std_col[chip_at, :]
    second = halves(sketch1)
    both = [jnp.concatenate(pair, axis=1) for pair in zip(first, second)]
    trailing = gram(second, both)
    gsend[:, :, 1] = pieces(trailing[:, :half])
    gsend[:, :, 2] = pieces(trailing[:, half:])
    send_gram(*waves[1])

    for c in range(2):
        rows = slice(c * portion, (c + 1) * portion)

        @pl.when(core == c)
        def _():
            sketch_out[:, :half] = sketch0[rows]
            sketch_out[:, half:] = sketch1[rows]


    def total_gram(wave):
        number, start, count, _ = waves[wave]
        at = pl.ds(start, count)
        mine = core * g_owners + g_index[wave]
        grecv[chip, at] = gsend[core, g_index[wave], at]
        wait_bytes(grecv.at[pl.ds(0, chips - 1), at], recv_sems.at[number])
        gfull[mine, at] = jnp.sum(grecv[:, at], axis=0)

        def share(step):
            to = (step % n_obs, step // n_obs)
            own = gfull.at[mine, at]
            pl.when((o != to[0]) | (f != to[1]))(
                lambda: send(own, own, number + 2, to) and None
            )

        each(0, n_obs * n_flux, share)

    pl.when(g_mine[0])(lambda: total_gram(0))
    pl.when(g_mine[1])(lambda: total_gram(1))

    def arrived(wave):
        number, start, count, _ = waves[wave]
        at = pl.ds(start, count)

        @pl.when(g_mine[wave])
        def _():
            wait_bytes(gfull.at[pl.ds(0, 2 * g_owners - 1), at], recv_sems.at[number + 2])

        @pl.when(jnp.logical_not(g_mine[wave]))
        def _():
            wait_bytes(gfull.at[:, at], recv_sems.at[number + 2])

    each(1, n_obs, lambda step: wait_bytes(jrecv.at[0], send_sems.at[2]))
    for b in range(blocks):
        for j in range(w_owners):
            pl.when(w_index != j)(lambda b=b: wait_bytes(fsend.at[b, 0], send_sems.at[b]))
        pl.when(w_mine)(
            lambda b=b: each(
                1, chips * (1 + b), lambda step: wait_bytes(wbuf.at[b, 0], send_sems.at[3 + b])
            )
        )
    across.wait_send()
    for wave, (number, start, count, _) in enumerate(waves):
        piece = gfull.at[0, pl.ds(start, count)]
        each(0, g_owners - 1, lambda step: wait_bytes(piece, send_sems.at[number]))
        pl.when(jnp.logical_not(g_mine[wave]))(lambda: wait_bytes(piece, send_sems.at[number]))

    arrived(0)
    work[...] = factor(gfull[:, 0].reshape(half, half))
    arrived(1)
    for wave, (number, start, count, _) in enumerate(waves):
        piece = gfull.at[0, pl.ds(start, count)]

        @pl.when(g_mine[wave])
        def _():
            each(1, 2 * chips, lambda step: wait_bytes(piece, send_sems.at[number + 2]))

    inverse = work[...]
    sketch = sketch_out[...]

    cross = product(gfull[:, 1].reshape(half, half), inverse, ((1,), (1,)))
    rest = gfull[:, 2].reshape(half, half) - product(cross, cross, ((1,), (1,)))
    first = product(sketch[:, :half], inverse, ((1,), (1,)))
    basis_out[:, :half] = first * scale
    basis_out[:, half:] = (sketch[:, half:] - product(first, cross, ((1,), (1,)))) * scale
    inverse_out[...] = factor(rest)


def finish(sketch, basis, inverse, sketch_out, basis_out):
    half = inverse.shape[0]
    sketch_out[...] = sketch[...]
    basis_out[:, :half] = basis[:, :half]
    basis_out[:, half:] = product(basis[:, half:], inverse[...], ((1,), (1,)))


def body(jacobian, probes, prior_std, obs_weight):
    blocks, flux_local, probe_count = probes.shape
    obs_local = jacobian.shape[0]
    n_obs, n_flux = lax.axis_size("obs"), lax.axis_size("flux")
    width = blocks * probe_count
    half = width // 2
    portion = flux_local // n_obs
    n_y = n_obs // 2
    chips = n_y * n_flux
    w_rows = max(16, 2 * obs_local // n_flux)
    w_owners = obs_local // w_rows
    g_owners = half // 2 // TILE
    scale = math.sqrt(flux_local * n_flux)
    vmem = pl.BlockSpec(memory_space=pltpu.VMEM)
    out = jax.ShapeDtypeStruct((portion, width), F32)
    operands = (jacobian, probes, prior_std.reshape(1, -1), obs_weight.reshape(1, -1))
    sketch, basis, inverse = pl.pallas_call(
        functools.partial(kernel, (n_obs, n_flux), scale),
        out_shape=(out, out, jax.ShapeDtypeStruct((half, half), F32)),
        in_specs=[pl.BlockSpec(memory_space=pl.ANY)] * 4,
        out_specs=(vmem, vmem, vmem),
        scratch_shapes=[
            pltpu.VMEM(jacobian.shape, BF16),
            pltpu.VMEM(probes.shape, BF16),
            pltpu.VMEM((1, flux_local), F32),
            pltpu.VMEM((1, obs_local), F32),
            pltpu.SemaphoreType.DMA((5,)),
            pltpu.VMEM((flux_local, LANES), F32),
            pltpu.VMEM((obs_local, LANES), F32),
            pltpu.VMEM((flux_local, obs_local), BF16),
            pltpu.VMEM((n_obs, 2 * portion, obs_local), BF16),
            pltpu.VMEM((blocks, w_owners, w_rows, half), F32),
            pltpu.VMEM((blocks, n_flux, w_rows, half), F32),
            pltpu.VMEM((blocks, 2 * n_y * w_owners, w_rows, half), BF16),
            pltpu.VMEM((2, g_owners, 3, TILE, half), F32),
            pltpu.VMEM((chips, 3, TILE, half), F32),
            pltpu.VMEM((2 * g_owners, 3, TILE, half), F32),
            pltpu.VMEM((half, half), F32),
            pltpu.SemaphoreType.REGULAR,
            pltpu.SemaphoreType.DMA((11,)),
            pltpu.SemaphoreType.DMA((11,)),
        ],
        compiler_params=pltpu.CompilerParams(
            collective_id=0, has_side_effects=True, vmem_limit_bytes=24 << 20
        ),
    )(*[pltpu.with_memory_space_constraint(x, pltpu.HBM) for x in operands])
    return pl.pallas_call(
        finish,
        out_shape=(out, out),
        in_specs=[vmem] * 3,
        out_specs=(vmem, vmem),
        compiler_params=pltpu.CompilerParams(vmem_limit_bytes=8 << 20),
    )(sketch, basis, inverse)


def solution(mesh):
    in_specs = (P("obs", "flux"), P(None, "flux", None), P("flux"), P("obs"))
    out_specs = (P(("flux", "obs"), None), P(("flux", "obs"), None))
    return jax.shard_map(body, mesh=mesh, in_specs=in_specs, out_specs=out_specs, check_vma=False)
```
